256 devices in a mesh: space: 8 (over x, core), snap: 32 (over y, z).
Axes of the slice: x: 4, y: 4, z: 8, core: 2. Of those that a mesh axis runs over, the one named last changes fastest.
Arguments:
- velocity: bfloat16 [256, 3, 16, 32, 128], P('snap', None, 'space'), may hold values from -40 to 40
- block_id: int32 [16, 32, 128], P('space'), may hold values from 0 to 7
- metric: float32 [8, 3], replicated, may hold values from 0.5 to 2
- leaf_rot: float32 [32, 8, 16], P('snap'), may hold values from -2 to 2
- merge_rot: float32 [31, 32, 16], replicated, may hold values from -1 to 1
- merge_order: int32 [31], replicated, may hold values from 0 to 1
- ref_cell: int32 [16], replicated, may hold values from 0 to 196607
Outputs:
- modes: float32 [16, 3, 16, 4096], P(None, None, 'space', 'snap')
The draws below stay inside these ranges and needn't reach their ends.
All inputs are finite; a program needn't handle non-finite values.
Results may differ from the reference program's by a relative error of at most 0.0003.
Values may be sent and summed in bfloat16 or wider, within the bound.
No kernel may reach another device: no remote copies, remote signals or barrier semaphores. Data moves between devices by JAX's collectives and lax.ppermute only.
A program may use at most 64 MiB of HBM per device.

```python
import math
import jax
import jax.numpy as jnp
from jax import lax

S = 8
NX = 32
NZ = 128
R = 16
NBLK = 8
SNAPS = 256
NY = 16
LEVELS = 5
NODES = 31
N_SNAP = 32


def draw_velocity(key, part):
    key_base = jax.random.fold_in(key, 11)
    key_cells = jax.random.fold_in(key, 12)
    shape = (SNAPS, 3, NY, NX, NZ)
    wall_pos = (jnp.arange(NY, dtype=jnp.float32) + 0.5) / NY
    profile = (1.0 + 2.0 * wall_pos).reshape(1, 1, NY, 1, 1)
    cell_scale = 0.3 * 10.0 ** jax.random.uniform(key_cells, (1, 3, NY, NX, NZ), jnp.float32)
    base = jnp.clip(jax.random.normal(key_base, shape, jnp.float32), -4.0, 4.0)
    field = base * cell_scale * profile
    return field.astype(jnp.bfloat16)


def set_ends(values, key, least, top_value):
    longest = values.shape.index(max(values.shape))
    spots = []
    for shift in (0, 1):
        where = [jax.random.randint(jax.random.fold_in(key, axis), (), 0, length) for axis, length in enumerate(values.shape)]
        where[longest] = (where[longest] + shift) % values.shape[longest]
        spots.append(tuple(where))
    return values.at[spots[0]].set(least).at[spots[1]].set(top_value)


def shard_levels(rng, dims, split, low, high):
    def one(axis_at, blocks):
        steps = jax.random.uniform(jax.random.fold_in(jax.random.fold_in(rng, 6), axis_at), (blocks,), jnp.float32, low / len(split), high / len(split))
        return jnp.repeat(jnp.exp(steps), dims[axis_at] // blocks).reshape((-1,) + (1,) * (len(dims) - axis_at - 1))

    level = one(*split[0])
    for cut in split[1:]:
        level = level * one(*cut)
    return level


def centred(stream_key, shape, deviation, limit, pieces=(), kind=jnp.bfloat16):
    result = deviation * jax.random.normal(stream_key, shape, jnp.float32)
    if pieces:
        result = result * shard_levels(stream_key, shape, pieces, -0.22, 0.18)
    return jnp.clip(result, -limit, limit).astype(kind)


def setup_inputs(seed: int = 0) -> dict:
    splits = jax.random.split(jax.random.key(seed), 8)
    velocity = draw_velocity(jax.random.fold_in(splits[7], 71), 0)
    block_id = set_ends(jax.random.randint(splits[1], (NY, NX, NZ), 0, NBLK), jax.random.fold_in(splits[1], 1), 0, NBLK - 1).astype(jnp.int32)
    metric = jnp.clip(jnp.exp(jax.random.uniform(splits[2], (NBLK, 3), jnp.float32, math.log(0.5), math.log(2.0))), 0.5, 2.0)
    leaf_rot = centred(splits[3], (N_SNAP, S, R), S ** -0.5, 2.0, ((0, 32),), jnp.float32)
    merge_rot = centred(splits[4], (NODES, 2 * R, R), (2 * R) ** -0.5, 1.0, (), jnp.float32)
    merge_order = set_ends(jax.random.randint(splits[5], (NODES,), 0, 2), jax.random.fold_in(splits[5], 1), 0, 1).astype(jnp.int32)
    ref_cell = set_ends(jax.random.randint(splits[6], (R,), 0, 3 * NY * NX * NZ), jax.random.fold_in(splits[6], 1), 0, (3 * NY * NX * NZ) - 1).astype(jnp.int32)
    return {"velocity": velocity, "block_id": block_id, "metric": metric, "leaf_rot": leaf_rot, "merge_rot": merge_rot, "merge_order": merge_order, "ref_cell": ref_cell}


HIGHEST = lax.Precision.HIGHEST

def along_x(field, spacing):
    return spacing[0] * (jnp.roll(field, -1, axis=2) - jnp.roll(field, 1, axis=2)) * 0.5

def along_z(field, spacing):
    return spacing[2] * (jnp.roll(field, -1, axis=3) - jnp.roll(field, 1, axis=3)) * 0.5

def along_y(field, spacing):
    padded = jnp.pad(field, ((0, 0), (1, 1), (0, 0), (0, 0)))
    return spacing[1] * (padded[:, 2:] - padded[:, :-2]) * 0.5

def vorticity_of(vel_block, spacing):
    vel_u = vel_block[:, 0]
    vel_v = vel_block[:, 1]
    vel_w = vel_block[:, 2]
    omega_x = along_y(vel_w, spacing) - along_z(vel_v, spacing)
    omega_y = along_z(vel_u, spacing) - along_x(vel_w, spacing)
    omega_z = along_x(vel_v, spacing) - along_y(vel_u, spacing)
    return jnp.stack([omega_x, omega_y, omega_z], axis=1)

def reference(velocity, block_id, metric, leaf_rot, merge_rot, merge_order, ref_cell):
    spacing = jnp.moveaxis(metric[block_id], -1, 0)
    rank = leaf_rot.shape[2]

    def leaf_block(group):
        vel_block = velocity[group * S:(group + 1) * S].astype(jnp.float32)
        omega = vorticity_of(vel_block, spacing).reshape(S, -1)
        return jnp.dot(leaf_rot[group].T, omega, precision=HIGHEST, preferred_element_type=jnp.float32)

    def node_block(tree_level, node_k):
        if tree_level < 0:
            return leaf_block(node_k)
        left_child = node_block(tree_level - 1, 2 * node_k)
        right_child = node_block(tree_level - 1, 2 * node_k + 1)
        node_id = N_SNAP - (N_SNAP >> tree_level) + node_k
        rotation = merge_rot[node_id]
        order_bit = merge_order[node_id]
        first = jnp.where(order_bit == 0, left_child, right_child)
        second = jnp.where(order_bit == 0, right_child, left_child)
        merged = jnp.dot(rotation[:rank].T, first, precision=HIGHEST, preferred_element_type=jnp.float32)
        merged = merged + jnp.dot(rotation[rank:].T, second, precision=HIGHEST, preferred_element_type=jnp.float32)
        gram_total = jnp.dot(merged, merged.T, precision=HIGHEST, preferred_element_type=jnp.float32)
        scale = (jnp.trace(gram_total) + 1e-06) / rank
        factor = 1.5 * jnp.eye(rank, dtype=jnp.float32) - 0.5 * gram_total / scale
        return jnp.dot(factor.T, merged, precision=HIGHEST, preferred_element_type=jnp.float32)
    root = node_block(LEVELS - 1, 0)
    norm_sq = lax.optimization_barrier(jnp.sum(root * root, axis=1))
    floor_value = 0.5 * jnp.sqrt(norm_sq / (3 * NY * NX * NZ) + 1e-06)
    value = jnp.take_along_axis(root, ref_cell.astype(jnp.int32)[:, None], axis=1)[:, 0]
    sign = value / jnp.maximum(jnp.abs(value), floor_value)
    modes = root * sign[:, None]
    return modes.reshape(rank, 3, NY, NX * NZ)
```

```python
import functools

import jax
import jax.numpy as jnp
from jax import lax
from jax.experimental import pallas as pl
from jax.experimental.pallas import tpu as pltpu
from jax.sharding import PartitionSpec as P

HIGHEST = lax.Precision.HIGHEST
VMEM = pl.BlockSpec(memory_space=pltpu.VMEM)
SMEM = pl.BlockSpec(memory_space=pltpu.SMEM)


def neighbours(cells, axis):
    count = lax.axis_size(axis)
    head, tail = cells[:, :, 0], cells[:, :, -1]
    below = lax.ppermute(tail, axis, [(i, i + 1) for i in range(count - 1)])
    above = lax.ppermute(head, axis, [(i + 1, i) for i in range(count - 1)])
    return below, above


def mm(left, right):
    return lax.dot_general(
        left, right, (((1,), (0,)), ((), ())), precision=HIGHEST, preferred_element_type=jnp.float32
    )


def mm_t(left, right):
    return lax.dot_general(
        left, right, (((1,), (1,)), ((), ())), precision=HIGHEST, preferred_element_type=jnp.float32
    )


def curl_kernel(metric_ref, block_ref, vel_ref, below_ref, above_ref, out_ref):
    snaps, _, rows_y, cells_x, _ = vel_ref.shape
    per_x = 3 * rows_y * snaps
    blocks = metric_ref.shape[0]
    half = []
    for y in range(rows_y):
        ids = block_ref[y]
        trio = []
        for k in range(3):
            value = jnp.full(ids.shape, metric_ref[0, k], jnp.float32)
            for b in range(1, blocks):
                value = jnp.where(ids == b, metric_ref[b, k], value)
            trio.append(0.5 * value)
        half.append(trio)

    def diff_x(field):
        return pltpu.roll(field, cells_x - 1, 0) - pltpu.roll(field, 1, 0)

    def diff_z(field):
        return pltpu.roll(field, field.shape[1] - 1, 1) - pltpu.roll(field, 1, 1)

    for s in range(snaps):
        u = [vel_ref[s, 0, y].astype(jnp.float32) for y in range(rows_y)]
        v = [vel_ref[s, 1, y].astype(jnp.float32) for y in range(rows_y)]
        w = [vel_ref[s, 2, y].astype(jnp.float32) for y in range(rows_y)]
        u_all = [below_ref[s, 0].astype(jnp.float32)] + u + [above_ref[s, 0].astype(jnp.float32)]
        w_all = [below_ref[s, 1].astype(jnp.float32)] + w + [above_ref[s, 1].astype(jnp.float32)]
        for y in range(rows_y):
            hx, hy, hz = half[y]
            trio = (
                hy * (w_all[y + 2] - w_all[y]) - hz * diff_z(v[y]),
                hz * diff_z(u[y]) - hx * diff_x(w[y]),
                hx * diff_x(v[y]) - hy * (u_all[y + 2] - u_all[y]),
            )
            for c in range(3):
                out_ref[pl.ds((c * rows_y + y) * snaps + s, cells_x, stride=per_x), :] = trio[c]


def gram_kernel(ref_pos_ref, field_ref, out_ref):
    groups, fields, snaps, lanes = field_ref.shape
    total = groups * snaps
    columns = [field_ref[:, f].reshape(total, lanes) for f in range(fields)]
    field = jnp.concatenate(columns, axis=1)
    gram = mm_t(field, field)
    positions = ref_pos_ref[...]
    hot = (lax.broadcasted_iota(jnp.int32, (lanes, fields * lanes), 1) == positions).astype(jnp.float32)
    picked = mm_t(field, hot)
    row = lax.broadcasted_iota(jnp.int32, gram.shape, 0)
    col = lax.broadcasted_iota(jnp.int32, gram.shape, 1)
    diagonal = jnp.sum(jnp.where(row == col, gram, 0.0), axis=1, keepdims=True)
    lane = lax.broadcasted_iota(jnp.int32, picked.shape, 1)
    extra = jnp.where(lane == 16, diagonal, picked)
    h = total // 2
    row_h = lax.broadcasted_iota(jnp.int32, (h, h), 0)
    col_h = lax.broadcasted_iota(jnp.int32, (h, h), 1)
    mixed = jnp.where(row_h <= col_h, gram[:h, :h], gram[h:, h:])
    out_ref[: groups // 2, :8] = mixed.reshape(groups // 2, snaps, h)
    out_ref[groups // 2 :, :8] = gram[:h, h:].reshape(groups // 2, snaps, h)
    out_ref[:, 8:] = extra.reshape(groups, snaps, h)


def sum_spread_kernel(parts_ref, out_ref):
    total = jnp.sum(parts_ref[...], axis=0)
    for i in range(out_ref.shape[0]):
        out_ref[i] = total


def sum_leaf_spread_kernel(parts_ref, leaf_ref, out_ref):
    total = jnp.sum(parts_ref[...], axis=0)
    snaps = leaf_ref.shape[1]
    bottom = total[snaps:]
    leaf = jnp.concatenate(
        [jnp.zeros((snaps, 32), jnp.float32), leaf_ref[0], jnp.zeros((snaps, 80), jnp.float32)], axis=1
    )
    for i in range(out_ref.shape[0]):
        out_ref[i, :snaps] = total[:snaps]
        out_ref[i, snaps:] = bottom + leaf


def tile_rows(block, count):
    return jnp.concatenate([block] * count, axis=0) if count > 1 else block


def spread(weights, count, span, offset=0):
    wide = tile_rows(weights, count)
    row = lax.broadcasted_iota(jnp.int32, wide.shape, 0)
    col = lax.broadcasted_iota(jnp.int32, wide.shape, 1)
    rank = weights.shape[0]
    return jnp.where(row // rank == col // span + offset, wide, 0.0)


def tree_kernel(cells_all, levels, table_ref, rot_ref, field_ref, out_ref):
    groups, fields, snaps, lanes = field_ref.shape
    total = groups * snaps
    h = total // 2
    packed = table_ref[:, :8].reshape(total, lanes)
    extra = table_ref[:, 8:].reshape(total, lanes)
    extra_t = extra.T
    picked = extra_t[:16]
    weights = extra_t[32:48]
    mixed = packed[:h]
    cross = packed[h:]
    mixed_t = mixed.T
    row = lax.broadcasted_iota(jnp.int32, (h, h), 0)
    col = lax.broadcasted_iota(jnp.int32, (h, h), 1)
    first = jnp.where(row <= col, mixed, mixed_t)
    last_diag = extra[h:, 16:17]
    last = jnp.where(row > col, mixed, jnp.where(row == col, last_diag, mixed_t))
    gram = jnp.concatenate(
        [jnp.concatenate([first, cross], axis=1), jnp.concatenate([cross.T, last], axis=1)], axis=0
    )
    row = lax.broadcasted_iota(jnp.int32, (total, total), 0)
    col = lax.broadcasted_iota(jnp.int32, (total, total), 1)
    rank = weights.shape[0]
    start = 0
    for level in range(levels):
        children = groups >> level
        width = children * rank
        base = start // lanes * lanes
        offset = (start - base) // rank
        cover = max(width, lanes)
        rot = rot_ref[:, base : base + cover]
        weights = mm(rot, spread(weights, cover // rank, total // children, offset))
        start += width
        nodes = children // 2
        span = total // nodes
        if nodes > 1:
            same = (row // span == col // span).astype(jnp.float32)
            local_gram = gram * same
        else:
            same = jnp.ones((total, total), jnp.float32)
            local_gram = gram
        moved = mm(weights, local_gram)
        own = jnp.sum(weights * moved, axis=0, keepdims=True)
        trace = mm(jnp.broadcast_to(own, (8, total)), same)[:1]
        wide = spread(weights, nodes, span)
        small = mm_t(moved, wide)
        turned = mm(small, wide)
        scale = (trace + 1e-06) / rank
        weights = 1.5 * weights - 0.5 * turned / scale
    norm_sq = jnp.sum(weights * mm(weights, gram), axis=1, keepdims=True)
    norm_sq = jnp.maximum(norm_sq, 0.0)
    value = jnp.sum(weights * picked, axis=1, keepdims=True)
    floor_value = 0.5 * jnp.sqrt(norm_sq / cells_all + 1e-06)
    weights = weights * (value / jnp.maximum(jnp.abs(value), floor_value))
    rows_y = out_ref.shape[2]
    for f in range(fields):
        modes = mm(weights, field_ref[:, f].reshape(total, lanes))
        out_ref[:, f // rows_y, f % rows_y, :] = modes


def call(kernel, shape, specs, *args, name):
    return pl.pallas_call(
        kernel,
        out_shape=jax.ShapeDtypeStruct(shape, jnp.float32),
        in_specs=specs,
        out_specs=VMEM,
        name=name,
        compiler_params=pltpu.CompilerParams(vmem_limit_bytes=48 * 2**20),
    )(*args)


def exchange(value, axis):
    return lax.all_to_all(value, axis, 0, 0, tiled=True)


def local(velocity, block_id, metric, leaf_rot, merge_rot, merge_order, ref_cell):
    snaps, _, rows_y, cells_x, cells_z = velocity.shape
    rank = leaf_rot.shape[2]
    groups = lax.axis_size("snap")
    slabs = lax.axis_size("space")
    snap_index = lax.axis_index("snap")
    space_index = lax.axis_index("space")
    fields = 3 * rows_y

    below, above = neighbours(velocity[:, 0::2], "space")
    swapped = jnp.where(merge_order[:, None, None] == 0, merge_rot, jnp.roll(merge_rot, rank, axis=1))
    rot = jnp.pad(jnp.transpose(swapped, (2, 0, 1)).reshape(rank, -1), ((0, 0), (0, 2 * rank)))
    plane = cells_x * cells_z
    rows_total = rows_y * slabs
    comp_of = ref_cell // (rows_total * plane)
    row_of = ref_cell // plane % rows_total - space_index * rows_y
    x_of = ref_cell % plane // cells_z
    here = (row_of >= 0) & (row_of < rows_y) & (x_of == snap_index)
    position = jnp.where(here, (comp_of * rows_y + row_of) * cells_z + ref_cell % cells_z, -1)
    position = jnp.pad(position, (0, cells_z - rank), constant_values=-1)[:, None]

    field = call(
        curl_kernel,
        (cells_x * fields * snaps, cells_z),
        [SMEM, VMEM, VMEM, VMEM, VMEM],
        metric,
        block_id,
        velocity,
        below,
        above,
        name="curl",
    )
    field = exchange(field.reshape(groups, fields * snaps, cells_z), "snap")
    field = field.reshape(groups, fields, snaps, cells_z)
    table = call(gram_kernel, (groups, 2 * snaps, cells_z), [VMEM, VMEM], position, field, name="gram")
    table = exchange(table, "snap")
    table = call(sum_spread_kernel, (slabs, 2 * snaps, cells_z), [VMEM], table, name="sum_snap")
    table = exchange(table, "space")
    table = call(
        sum_leaf_spread_kernel, (groups, 2 * snaps, cells_z), [VMEM, VMEM], table, leaf_rot, name="sum_space"
    )
    table = exchange(table, "snap")
    return call(
        functools.partial(tree_kernel, fields // 3 * plane * 3 * slabs, groups.bit_length() - 1),
        (rank, 3, rows_y, cells_z),
        [VMEM, VMEM, VMEM],
        table,
        rot,
        field,
        name="tree",
    )


def solution(mesh):
    placed = (
        P("snap", None, "space", None, None),
        P("space", None, None),
        P(),
        P("snap", None, None),
        P(),
        P(),
        P(),
    )
    return jax.shard_map(
        local, mesh=mesh, in_specs=placed, out_specs=P(None, None, "space", "snap"), check_vma=False
    )
```

```python
import functools

import jax
import jax.numpy as jnp
from jax import lax
from jax.experimental import pallas as pl
from jax.experimental.pallas import tpu as pltpu
from jax.sharding import PartitionSpec as P

HIGHEST = lax.Precision.HIGHEST
VMEM = pl.BlockSpec(memory_space=pltpu.VMEM)
SMEM = pl.BlockSpec(memory_space=pltpu.SMEM)


def mm(left, right):
    return lax.dot_general(
        left, right, (((1,), (0,)), ((), ())), precision=HIGHEST, preferred_element_type=jnp.float32
    )


def mm_t(left, right):
    return lax.dot_general(
        left, right, (((1,), (1,)), ((), ())), precision=HIGHEST, preferred_element_type=jnp.float32
    )


SLOTS = {(0, 0): 0, (2, 0): 1, (1, 0): 2, (1, 1): 3, (2, 1): 4, (0, 1): 5}


def pack_kernel(vel_ref, out_ref, rows_ref):
    snaps, comps, rows_y, cells_x, lanes = vel_ref.shape
    per_x = comps * rows_y * snaps
    for (c, y), slot in SLOTS.items():
        for s in range(snaps):
            rows_ref[pl.ds(slot * snaps + s, cells_x, stride=per_x), :] = vel_ref[s, c, y].astype(jnp.float32)
    out_ref[...] = rows_ref[...].reshape(cells_x, per_x, lanes).astype(out_ref.dtype)


def gram_kernel(metric_ref, block_ref, ref_pos_ref, own_ref, left_ref, right_ref, below_ref, above_ref, field_ref, out_ref):
    groups, per_x, lanes = own_ref.shape
    rows_y = block_ref.shape[0]
    fields = 3 * rows_y
    snaps = per_x // fields
    total = groups * snaps

    def rows(ref, slot):
        return ref[:, slot * snaps : (slot + 1) * snaps, :].astype(jnp.float32).reshape(total, lanes)

    def diff_z(field):
        return pltpu.roll(field, lanes - 1, 1) - pltpu.roll(field, 1, 1)

    def diff_x(c, y):
        slot = SLOTS[c, y] - 1
        return rows(right_ref, slot) - rows(left_ref, slot)

    u, v, w = ([rows(own_ref, SLOTS[c, y]) for y in range(rows_y)] for c in range(3))
    u_all = [rows(below_ref, 1)] + u + [rows(above_ref, 0)]
    w_all = [rows(below_ref, 0)] + w + [rows(above_ref, 1)]
    for y in range(rows_y):
        ids = block_ref[y]
        half = []
        for k in range(3):
            value = jnp.full(ids.shape, metric_ref[0, k], jnp.float32)
            for b in range(1, metric_ref.shape[0]):
                value = jnp.where(ids == b, metric_ref[b, k], value)
            half.append(0.5 * value)
        hx, hy, hz = half
        field_ref[:, y * lanes : (y + 1) * lanes] = hy * (w_all[y + 2] - w_all[y]) - hz * diff_z(v[y])
        at = rows_y + y
        field_ref[:, at * lanes : (at + 1) * lanes] = hz * diff_z(u[y]) - hx * diff_x(2, y)
        at = 2 * rows_y + y
        field_ref[:, at * lanes : (at + 1) * lanes] = hx * diff_x(1, y) - hy * (u_all[y + 2] - u_all[y])

    field = field_ref[...]
    gram = mm_t(field, field)
    positions = ref_pos_ref[...]
    hot = (lax.broadcasted_iota(jnp.int32, (lanes, fields * lanes), 1) == positions).astype(jnp.float32)
    picked = mm_t(field, hot)
    row = lax.broadcasted_iota(jnp.int32, gram.shape, 0)
    col = lax.broadcasted_iota(jnp.int32, gram.shape, 1)
    diagonal = jnp.sum(jnp.where(row == col, gram, 0.0), axis=1, keepdims=True)
    lane = lax.broadcasted_iota(jnp.int32, picked.shape, 1)
    extra = jnp.where(lane == 16, diagonal, picked)
    h = total // 2
    row_h = lax.broadcasted_iota(jnp.int32, (h, h), 0)
    col_h = lax.broadcasted_iota(jnp.int32, (h, h), 1)
    mixed = jnp.where(row_h <= col_h, gram[:h, :h], gram[h:, h:])
    out_ref[: groups // 2, :8] = mixed.reshape(groups // 2, snaps, h)
    out_ref[groups // 2 :, :8] = gram[:h, h:].reshape(groups // 2, snaps, h)
    out_ref[:, 8:] = extra.reshape(groups, snaps, h)


def sum_spread_kernel(parts_ref, out_ref):
    total = jnp.sum(parts_ref[...], axis=0)
    for i in range(out_ref.shape[0]):
        out_ref[i] = total


def sum_leaf_spread_kernel(parts_ref, leaf_ref, out_ref):
    total = jnp.sum(parts_ref[...], axis=0)
    snaps = leaf_ref.shape[1]
    bottom = total[snaps:]
    leaf = jnp.concatenate(
        [jnp.zeros((snaps, 32), jnp.float32), leaf_ref[0], jnp.zeros((snaps, 80), jnp.float32)], axis=1
    )
    for i in range(out_ref.shape[0]):
        out_ref[i, :snaps] = total[:snaps]
        out_ref[i, snaps:] = bottom + leaf


def tile_rows(block, count):
    return jnp.concatenate([block] * count, axis=0) if count > 1 else block


def spread(weights, count, span, offset=0):
    wide = tile_rows(weights, count)
    row = lax.broadcasted_iota(jnp.int32, wide.shape, 0)
    col = lax.broadcasted_iota(jnp.int32, wide.shape, 1)
    rank = weights.shape[0]
    return jnp.where(row // rank == col // span + offset, wide, 0.0)


def tree_kernel(cells_all, levels, table_ref, rot_ref, field_ref, out_ref):
    groups, rows_all, lanes = table_ref.shape
    snaps = rows_all // 2
    total = groups * snaps
    h = total // 2
    packed = table_ref[:, :8].reshape(total, lanes)
    extra = table_ref[:, 8:].reshape(total, lanes)
    extra_t = extra.T
    picked = extra_t[:16]
    weights = extra_t[32:48]
    mixed = packed[:h]
    cross = packed[h:]
    mixed_t = mixed.T
    row = lax.broadcasted_iota(jnp.int32, (h, h), 0)
    col = lax.broadcasted_iota(jnp.int32, (h, h), 1)
    first = jnp.where(row <= col, mixed, mixed_t)
    last_diag = extra[h:, 16:17]
    last = jnp.where(row > col, mixed, jnp.where(row == col, last_diag, mixed_t))
    gram = jnp.concatenate(
        [jnp.concatenate([first, cross], axis=1), jnp.concatenate([cross.T, last], axis=1)], axis=0
    )
    row = lax.broadcasted_iota(jnp.int32, (total, total), 0)
    col = lax.broadcasted_iota(jnp.int32, (total, total), 1)
    rank = weights.shape[0]
    start = 0
    for level in range(levels):
        children = groups >> level
        width = children * rank
        base = start // lanes * lanes
        offset = (start - base) // rank
        cover = max(width, lanes)
        rot = rot_ref[:, base : base + cover]
        weights = mm(rot, spread(weights, cover // rank, total // children, offset))
        start += width
        nodes = children // 2
        span = total // nodes
        if nodes > 1:
            same = (row // span == col // span).astype(jnp.float32)
            local_gram = gram * same
        else:
            same = jnp.ones((total, total), jnp.float32)
            local_gram = gram
        moved = mm(weights, local_gram)
        own = jnp.sum(weights * moved, axis=0, keepdims=True)
        trace = mm(jnp.broadcast_to(own, (8, total)), same)[:1]
        wide = spread(weights, nodes, span)
        small = mm_t(moved, wide)
        turned = mm(small, wide)
        scale = (trace + 1e-06) / rank
        weights = 1.5 * weights - 0.5 * turned / scale
    norm_sq = jnp.sum(weights * mm(weights, gram), axis=1, keepdims=True)
    norm_sq = jnp.maximum(norm_sq, 0.0)
    value = jnp.sum(weights * picked, axis=1, keepdims=True)
    floor_value = 0.5 * jnp.sqrt(norm_sq / cells_all + 1e-06)
    weights = weights * (value / jnp.maximum(jnp.abs(value), floor_value))
    rows_y = out_ref.shape[2]
    modes = mm(weights, field_ref[...])
    for f in range(3 * rows_y):
        out_ref[:, f // rows_y, f % rows_y, :] = modes[:, f * lanes : (f + 1) * lanes]


def call(kernel, shapes, specs, *args, name, scratch=()):
    outs = jax.tree.map(lambda _: VMEM, shapes)
    return pl.pallas_call(
        kernel,
        out_shape=shapes,
        in_specs=specs,
        out_specs=outs,
        scratch_shapes=scratch,
        name=name,
        compiler_params=pltpu.CompilerParams(vmem_limit_bytes=48 * 2**20),
    )(*args)


def f32(*shape):
    return jax.ShapeDtypeStruct(shape, jnp.float32)


def exchange(value, axis):
    return lax.all_to_all(value, axis, 0, 0, tiled=True)


def local(velocity, block_id, metric, leaf_rot, merge_rot, merge_order, ref_cell):
    snaps, _, rows_y, cells_x, cells_z = velocity.shape
    rank = leaf_rot.shape[2]
    groups = lax.axis_size("snap")
    slabs = lax.axis_size("space")
    snap_index = lax.axis_index("snap")
    space_index = lax.axis_index("space")
    fields = 3 * rows_y

    swapped = jnp.where(merge_order[:, None, None] == 0, merge_rot, jnp.roll(merge_rot, rank, axis=1))
    rot = jnp.pad(jnp.transpose(swapped, (2, 0, 1)).reshape(rank, -1), ((0, 0), (0, 2 * rank)))
    plane = cells_x * cells_z
    rows_total = rows_y * slabs
    comp_of = ref_cell // (rows_total * plane)
    row_of = ref_cell // plane % rows_total - space_index * rows_y
    x_of = ref_cell % plane // cells_z
    here = (row_of >= 0) & (row_of < rows_y) & (x_of == snap_index)
    position = jnp.where(here, (comp_of * rows_y + row_of) * cells_z + ref_cell % cells_z, -1)
    position = jnp.pad(position, (0, cells_z - rank), constant_values=-1)[:, None]

    ids = lax.dynamic_slice_in_dim(block_id, snap_index, 1, 1)

    per_x = fields * snaps
    packed = call(
        pack_kernel,
        jax.ShapeDtypeStruct((cells_x, per_x, cells_z), velocity.dtype),
        [VMEM],
        velocity,
        name="pack",
        scratch=[pltpu.VMEM((cells_x * per_x, cells_z), jnp.float32)],
    )
    own = exchange(packed, "snap")
    inner = own[:, snaps : 5 * snaps]
    left = lax.ppermute(inner, "snap", [(i, (i + 1) % groups) for i in range(groups)])
    right = lax.ppermute(inner, "snap", [((i + 1) % groups, i) for i in range(groups)])
    below = lax.ppermute(own[:, 4 * snaps :], "space", [(i, i + 1) for i in range(slabs - 1)])
    above = lax.ppermute(own[:, : 2 * snaps], "space", [(i + 1, i) for i in range(slabs - 1)])
    field, table = call(
        gram_kernel,
        (f32(groups * snaps, fields * cells_z), f32(groups, 2 * snaps, cells_z)),
        [SMEM] + [VMEM] * 7,
        metric,
        ids,
        position,
        own,
        left,
        right,
        below,
        above,
        name="gram",
    )
    table = exchange(table, "snap")
    table = call(sum_spread_kernel, f32(slabs, 2 * snaps, cells_z), [VMEM], table, name="sum_snap")
    table = exchange(table, "space")
    table = call(
        sum_leaf_spread_kernel, f32(groups, 2 * snaps, cells_z), [VMEM, VMEM], table, leaf_rot, name="sum_space"
    )
    table = exchange(table, "snap")
    return call(
        functools.partial(tree_kernel, fields * plane * slabs, groups.bit_length() - 1),
        f32(rank, 3, rows_y, cells_z),
        [VMEM, VMEM, VMEM],
        table,
        rot,
        field,
        name="tree",
    )


def solution(mesh):
    placed = (
        P("snap", None, "space", None, None),
        P("space", None, None),
        P(),
        P("snap", None, None),
        P(),
        P(),
        P(),
    )
    return jax.shard_map(
        local, mesh=mesh, in_specs=placed, out_specs=P(None, None, "space", "snap"), check_vma=False
    )
```

```python
import functools

import jax
import jax.numpy as jnp
from jax import lax
from jax.experimental import pallas as pl
from jax.experimental.pallas import tpu as pltpu
from jax.sharding import PartitionSpec as P

HIGHEST = lax.Precision.HIGHEST
VMEM = pl.BlockSpec(memory_space=pltpu.VMEM)
SNAP = ("y", "z")
WIDE = ("space", "y")


BF16 = jnp.bfloat16


def split3(value):
    high = value.astype(BF16)
    rest = value - high.astype(jnp.float32)
    middle = rest.astype(BF16)
    low = (rest - middle.astype(jnp.float32)).astype(BF16)
    return high, middle, low


def dot(left, right, transposed=False):
    dims = (((1,), (1 if transposed else 0,)), ((), ()))
    return lax.dot_general(left, right, dims, preferred_element_type=jnp.float32)


def mm3(left, right, transposed=False):
    rows = left[0].shape[0]
    high = dot(jnp.concatenate(left, axis=0), right[0], transposed)
    middle = dot(jnp.concatenate(left[:2], axis=0), right[1], transposed)
    low = dot(left[0], right[2], transposed)
    small = low + middle[rows:] + high[2 * rows :]
    return small + (middle[:rows] + high[rows : 2 * rows]) + high[:rows]


SLOTS = {(0, 0): 0, (2, 0): 1, (1, 0): 2, (1, 1): 3, (2, 1): 4, (0, 1): 5}


def pack_kernel(vel_hbm, out_hbm, vel_ref, rows_ref, out_ref, in_sems, out_sems):
    snaps, comps, rows_y, cells_x, lanes = vel_hbm.shape
    arrivals, leaving = {}, []
    for (c, y), slot in SLOTS.items():
        arrivals[slot] = pltpu.make_async_copy(vel_hbm.at[:, c, y], vel_ref.at[slot], in_sems.at[slot])
        arrivals[slot].start()
    for slot, copy in arrivals.items():
        copy.wait()
        for s in range(snaps):
            rows_ref[slot, pl.ds(s, cells_x, stride=snaps), :] = vel_ref[slot, s].astype(jnp.float32)
        out_ref[slot] = rows_ref[slot].reshape(cells_x, snaps, lanes).astype(out_ref.dtype)
        target = out_hbm.at[:, pl.ds(slot * snaps, snaps)]
        leaving.append(pltpu.make_async_copy(out_ref.at[slot], target, out_sems.at[slot]))
        leaving[-1].start()
    for copy in leaving:
        copy.wait()


def gram_kernel(
    half_ref, ref_pos_ref, own_ref, left_ref, right_ref, below_ref, above_ref, leaf_ref,
    parts_ref, out_ref
):
    groups, per_x, lanes = own_ref.shape
    rows_y = half_ref.shape[0]
    fields = 3 * rows_y
    snaps = per_x // fields
    total = groups * snaps

    def rows(ref, slot):
        return ref[:, slot * snaps : (slot + 1) * snaps, :].astype(jnp.float32).reshape(total, lanes)

    def diff_z(field):
        return pltpu.roll(field, lanes - 1, 1) - pltpu.roll(field, 1, 1)

    def diff_x(c, y):
        slot = SLOTS[c, y] - 1
        return rows(right_ref, slot) - rows(left_ref, slot)

    u, v, w = ([rows(own_ref, SLOTS[c, y]) for y in range(rows_y)] for c in range(3))
    u_all = [rows(below_ref, 1)] + u + [rows(above_ref, 0)]
    w_all = [rows(below_ref, 0)] + w + [rows(above_ref, 1)]
    pieces = [None] * fields
    for y in range(rows_y):
        half = (half_ref[y, k : k + 1] for k in range(3))
        hx, hy, hz = half
        pieces[y] = hy * (w_all[y + 2] - w_all[y]) - hz * diff_z(v[y])
        pieces[rows_y + y] = hz * diff_z(u[y]) - hx * diff_x(2, y)
        pieces[2 * rows_y + y] = hx * diff_x(1, y) - hy * (u_all[y + 2] - u_all[y])
    for f, piece in enumerate(pieces):
        for i, part in enumerate(split3(piece)):
            parts_ref[i * total : (i + 1) * total, f * lanes : (f + 1) * lanes] = part

    high = dot(parts_ref[...], parts_ref[:total], True)
    middle = dot(parts_ref[: 2 * total], parts_ref[total : 2 * total], True)
    low = dot(parts_ref[:total], parts_ref[2 * total :], True)
    gram = low + middle[total:] + high[2 * total :]
    gram = gram + (middle[:total] + high[total : 2 * total]) + high[:total]
    positions = ref_pos_ref[...]
    hot = (lax.broadcasted_iota(jnp.int32, (lanes, fields * lanes), 1) == positions).astype(jnp.float32).astype(BF16)
    picked = dot(parts_ref[...], hot, True)
    picked = picked[:total] + picked[total : 2 * total] + picked[2 * total :]
    row = lax.broadcasted_iota(jnp.int32, gram.shape, 0)
    col = lax.broadcasted_iota(jnp.int32, gram.shape, 1)
    diagonal = jnp.sum(jnp.where(row == col, gram, 0.0), axis=1, keepdims=True)
    lane = lax.broadcasted_iota(jnp.int32, picked.shape, 1)
    extra = jnp.where(lane == 16, diagonal, picked)
    h = total // 2
    row_h = lax.broadcasted_iota(jnp.int32, (h, h), 0)
    col_h = lax.broadcasted_iota(jnp.int32, (h, h), 1)
    mixed = jnp.where(row_h <= col_h, gram[:h, :h], gram[h:, h:])
    out_ref[: groups // 2, :8] = mixed.reshape(groups // 2, snaps, h)
    out_ref[groups // 2 :, :8] = gram[:h, h:].reshape(groups // 2, snaps, h)
    out_ref[:, 8:] = extra.reshape(groups, snaps, h) + leaf_ref[...][None]


def sum_spread_kernel(parts_ref, out_ref):
    total = jnp.sum(parts_ref[...], axis=0)
    for i in range(out_ref.shape[0]):
        out_ref[i] = total


def start_kernel(parts_ref, children_ref, weights_ref, rotate_ref):
    snaps = parts_ref.shape[1] // 2
    rank, total = weights_ref.shape
    levels = rotate_ref.shape[1] // total + 1
    misc = parts_ref[:, snaps:].reshape(-1, parts_ref.shape[2]).T
    count = total // misc.shape[1]
    leaves = jnp.concatenate([misc[(2 + i) * rank : (3 + i) * rank] for i in range(count)], axis=1)
    tables = jnp.concatenate(split3(children_ref[...].T), axis=0)
    width = tables.shape[1]
    child = lax.broadcasted_iota(jnp.int32, (width, total), 0)
    snap = lax.broadcasted_iota(jnp.int32, (width, total), 1)
    first, span = 0, snaps
    for level in range(levels):
        chosen = (child == first + snap // span).astype(jnp.float32).astype(BF16)
        first, span = first + total // span, span * 2
        spread = dot(tables, chosen)
        size = spread.shape[0] // 3
        spread = spread[:size] + spread[size : 2 * size] + spread[2 * size :]
        if level:
            rotate_ref[:, (level - 1) * total : level * total] = spread
        else:
            weights_ref[...] = rotated(leaves, spread)


def rotated(weights, rotate_ref):
    rank = weights.shape[0]
    total = rotate_ref[:rank] * weights[:1]
    for a in range(1, rank):
        total = total + rotate_ref[a * rank : (a + 1) * rank] * weights[a : a + 1]
    return total


def tree_kernel(cells_all, table_ref, weights_ref, rotate_ref, parts_ref, out_ref):
    groups, rows_all, lanes = table_ref.shape
    snaps = rows_all // 2
    rank = weights_ref.shape[0]
    total = groups * snaps
    h = total // 2
    packed = table_ref[:, :snaps].reshape(total, lanes)
    extra = table_ref[:, snaps:].reshape(total, lanes)
    picked = extra.T[:rank]
    mixed = packed[:h]
    cross = packed[h:]
    mixed_t = mixed.T
    row = lax.broadcasted_iota(jnp.int32, (h, h), 0)
    col = lax.broadcasted_iota(jnp.int32, (h, h), 1)
    first = jnp.where(row <= col, mixed, mixed_t)
    last = jnp.where(row > col, mixed, jnp.where(row == col, extra[h:, rank : rank + 1], mixed_t))
    first = split3(first)
    last = split3(last)
    cross = split3(cross)

    def moved_by(left):
        lower = tuple(part[:, :h] for part in left)
        upper = tuple(part[:, h:] for part in left)
        begin = mm3(lower, first) + mm3(upper, cross, True)
        return jnp.concatenate([begin, mm3(lower, cross) + mm3(upper, last)], axis=1)

    row_all = lax.broadcasted_iota(jnp.int32, (total, total), 0)
    col_all = lax.broadcasted_iota(jnp.int32, (total, total), 1)
    weights = weights_ref[...]
    levels = groups.bit_length() - 1
    for level in range(levels):
        span = 2 * snaps << level
        if level:
            weights = rotated(weights, rotate_ref.at[:, (level - 1) * total : level * total])
        left = split3(weights)
        same = (row_all // span == col_all // span).astype(jnp.float32).astype(BF16)
        if span < total:
            inside = same[:h, :h]
            begin = mm3(tuple(part[:, :h] for part in left), tuple(part * inside for part in first))
            end = mm3(tuple(part[:, h:] for part in left), tuple(part * inside for part in last))
            moved = jnp.concatenate([begin, end], axis=1)
        else:
            moved = moved_by(left)
        own = jnp.sum(weights * moved, axis=0, keepdims=True)
        products = [weights[j : j + 1] * moved for j in range(rank)]
        products = jnp.concatenate(products + [jnp.broadcast_to(own, (rank, total))], axis=0)
        upper = products.astype(BF16)
        lower = (products - upper.astype(jnp.float32)).astype(BF16)
        count = products.shape[0]
        sums = dot(jnp.concatenate([upper, lower], axis=0), same)
        sums = sums[count:] + sums[:count]
        scale = (sums[rank * rank :] + 1e-06) / rank
        turned = sums[:rank] * weights[:1]
        for j in range(1, rank):
            turned = turned + sums[j * rank : (j + 1) * rank] * weights[j : j + 1]
        weights = 1.5 * weights - 0.5 * turned / scale
    norm_sq = jnp.sum(weights * moved_by(split3(weights)), axis=1, keepdims=True)
    norm_sq = jnp.maximum(norm_sq, 0.0)
    value = jnp.sum(weights * picked, axis=1, keepdims=True)
    floor_value = 0.5 * jnp.sqrt(norm_sq / cells_all + 1e-06)
    weights = weights * (value / jnp.maximum(jnp.abs(value), floor_value))
    rows_y = out_ref.shape[2]
    modes = mm3(split3(weights), tuple(parts_ref[i * total : (i + 1) * total] for i in range(3)))
    for f in range(3 * rows_y):
        out_ref[:, f // rows_y, f % rows_y, :] = modes[:, f * lanes : (f + 1) * lanes]


def call(kernel, shapes, specs, *args, name, scratch=()):
    outs = jax.tree.map(lambda _: VMEM, shapes)
    return pl.pallas_call(
        kernel,
        out_shape=shapes,
        in_specs=specs,
        out_specs=outs,
        scratch_shapes=scratch,
        name=name,
        compiler_params=pltpu.CompilerParams(vmem_limit_bytes=20 * 2**20),
    )(*args)


def f32(*shape):
    return jax.ShapeDtypeStruct(shape, jnp.float32)


def exchange(value, axis):
    return lax.all_to_all(value, axis, 0, 0, tiled=True)


def child_maps(merge_rot, merge_order):
    rank = merge_rot.shape[2]
    swapped = jnp.where(merge_order[:, None, None] == 0, merge_rot, jnp.roll(merge_rot, rank, axis=1))
    children = swapped.reshape(-1, rank * rank)
    return jnp.pad(children, ((0, -children.shape[0] % 128), (0, 0)))


def local(velocity, block_id, metric, leaf_rot, merge_rot, merge_order, ref_cell):
    snaps, _, rows_y, cells_x, cells_z = velocity.shape
    rank = leaf_rot.shape[2]
    groups = lax.axis_size(SNAP)
    slabs = lax.axis_size("space")
    snap_index = lax.axis_index(SNAP)
    space_index = lax.axis_index("space")
    fields = 3 * rows_y
    total = groups * snaps
    plane = cells_x * cells_z

    per_x = fields * snaps
    packed = pl.pallas_call(
        pack_kernel,
        out_shape=jax.ShapeDtypeStruct((cells_x, per_x, cells_z), velocity.dtype),
        in_specs=[pl.BlockSpec(memory_space=pl.ANY)],
        out_specs=pl.BlockSpec(memory_space=pl.ANY),
        scratch_shapes=[
            pltpu.VMEM((fields, snaps, cells_x, cells_z), velocity.dtype),
            pltpu.VMEM((fields, cells_x * snaps, cells_z), jnp.float32),
            pltpu.VMEM((fields, cells_x, snaps, cells_z), velocity.dtype),
            pltpu.SemaphoreType.DMA((fields,)),
            pltpu.SemaphoreType.DMA((fields,)),
        ],
        name="pack",
    )(velocity)
    own = exchange(packed, SNAP)

    children = child_maps(merge_rot, merge_order)
    rows_total = rows_y * slabs
    comp_of = ref_cell // (rows_total * plane)
    row_of = ref_cell // plane % rows_total - space_index * rows_y
    x_of = ref_cell % plane // cells_z
    here = (row_of >= 0) & (row_of < rows_y) & (x_of == snap_index)
    position = jnp.where(here, (comp_of * rows_y + row_of) * cells_z + ref_cell % cells_z, -1)
    position = jnp.pad(position, (0, cells_z - rank), constant_values=-1)[:, None]
    ids = lax.dynamic_index_in_dim(block_id, snap_index, 1, keepdims=False)
    half = 0.5 * sum(
        jnp.where(ids[:, None] == b, metric[b][None, :, None], 0.0) for b in range(metric.shape[0])
    )
    slot = jnp.arange(cells_z, dtype=jnp.int32) // rank - 2
    leaf_here = (slot == lax.axis_index("y")) & (space_index == 0)
    leaf_tile = jnp.where(leaf_here, jnp.tile(leaf_rot[0], (1, cells_z // rank)), 0.0)

    own, children, position, half, leaf_tile = lax.optimization_barrier((own, children, position, half, leaf_tile))
    inner = own[:, snaps : 5 * snaps]
    below = lax.ppermute(own[:, 4 * snaps :], "space", [(i, i + 1) for i in range(slabs - 1)])
    above = lax.ppermute(own[:, : 2 * snaps], "space", [(i + 1, i) for i in range(slabs - 1)])
    left = lax.ppermute(inner, SNAP, [(i, (i + 1) % groups) for i in range(groups)])
    right = lax.ppermute(inner, SNAP, [((i + 1) % groups, i) for i in range(groups)])
    field_parts, table = call(
        gram_kernel,
        (jax.ShapeDtypeStruct((3 * total, fields * cells_z), BF16), f32(groups, 2 * snaps, cells_z)),
        [VMEM] * 8,
        half,
        position,
        own,
        left,
        right,
        below,
        above,
        leaf_tile,
        name="gram",
    )
    table = exchange(table, WIDE)
    table = call(sum_spread_kernel, f32(lax.axis_size("z"), 2 * snaps, cells_z), [VMEM], table, name="sum_wide")
    parts, children = lax.optimization_barrier((exchange(table, "z"), children))
    table = call(sum_spread_kernel, f32(groups, 2 * snaps, cells_z), [VMEM], parts, name="sum_z")
    table = exchange(table, WIDE)
    levels = groups.bit_length() - 1
    weights, rotate = call(
        start_kernel,
        (f32(rank, total), f32(rank * rank, (levels - 1) * total)),
        [VMEM, VMEM],
        parts,
        children,
        name="start",
    )
    return call(
        functools.partial(tree_kernel, fields * plane * slabs),
        f32(rank, 3, rows_y, cells_z),
        [VMEM] * 4,
        table,
        weights,
        rotate,
        field_parts,
        name="tree",
    )


def solution(mesh):
    torus = jax.sharding.Mesh(mesh.devices.reshape(mesh.shape["space"], 4, -1), ("space", "y", "z"))
    placed = (
        P(SNAP, None, "space", None, None),
        P("space", None, None),
        P(),
        P(SNAP, None, None),
        P(),
        P(),
        P(),
    )
    return jax.shard_map(
        local, mesh=torus, in_specs=placed, out_specs=P(None, None, "space", SNAP), check_vma=False
    )
```

```python
import functools

import jax
import jax.numpy as jnp
from jax import lax
from jax.experimental import pallas as pl
from jax.experimental.pallas import tpu as pltpu
from jax.sharding import PartitionSpec as P

HIGHEST = lax.Precision.HIGHEST
VMEM = pl.BlockSpec(memory_space=pltpu.VMEM)
SNAP = ("y", "z")
WIDE = ("space", "y")


BF16 = jnp.bfloat16


def split3(value):
    high = value.astype(BF16)
    rest = value - high.astype(jnp.float32)
    middle = rest.astype(BF16)
    low = (rest - middle.astype(jnp.float32)).astype(BF16)
    return high, middle, low


def dot(left, right, transposed=False):
    dims = (((1,), (1 if transposed else 0,)), ((), ()))
    return lax.dot_general(left, right, dims, preferred_element_type=jnp.float32)


def mm3(left, right, transposed=False):
    rows = left[0].shape[0]
    high = dot(jnp.concatenate(left, axis=0), right[0], transposed)
    middle = dot(jnp.concatenate(left[:2], axis=0), right[1], transposed)
    low = dot(left[0], right[2], transposed)
    small = low + middle[rows:] + high[2 * rows :]
    return small + (middle[:rows] + high[rows : 2 * rows]) + high[:rows]


SLOTS = {(0, 0): 0, (2, 0): 1, (1, 0): 2, (1, 1): 3, (2, 1): 4, (0, 1): 5}


def pack_kernel(vel_hbm, out_hbm, vel_ref, rows_ref, out_ref, in_sems, out_sems):
    snaps, comps, rows_y, cells_x, lanes = vel_hbm.shape
    arrivals, leaving = {}, []
    for (c, y), slot in SLOTS.items():
        arrivals[slot] = pltpu.make_async_copy(vel_hbm.at[:, c, y], vel_ref.at[slot], in_sems.at[slot])
        arrivals[slot].start()
    for slot, copy in arrivals.items():
        copy.wait()
        for s in range(snaps):
            rows_ref[slot, pl.ds(s, cells_x, stride=snaps), :] = vel_ref[slot, s].astype(jnp.float32)
        out_ref[slot] = rows_ref[slot].reshape(cells_x, snaps, lanes).astype(out_ref.dtype)
        target = out_hbm.at[:, pl.ds(slot * snaps, snaps)]
        leaving.append(pltpu.make_async_copy(out_ref.at[slot], target, out_sems.at[slot]))
        leaving[-1].start()
    for copy in leaving:
        copy.wait()


def gram_kernel(
    half_ref, ref_pos_ref, own_ref, left_ref, right_ref, chip_ref, next_ref, even_ref, leaf_ref,
    parts_ref, out_ref
):
    groups, per_x, lanes = own_ref.shape
    rows_y = half_ref.shape[0]
    fields = 3 * rows_y
    snaps = per_x // fields
    total = groups * snaps

    def rows(ref, slot):
        return ref[:, slot * snaps : (slot + 1) * snaps, :].astype(jnp.float32).reshape(total, lanes)

    def diff_z(field):
        return pltpu.roll(field, lanes - 1, 1) - pltpu.roll(field, 1, 1)

    def diff_x(c, y):
        slot = SLOTS[c, y] - 1
        return rows(right_ref, slot) - rows(left_ref, slot)

    u, v, w = ([rows(own_ref, SLOTS[c, y]) for y in range(rows_y)] for c in range(3))
    even = even_ref[:1] > 0
    chip = [rows(chip_ref, i) for i in range(2)]
    beyond = [rows(next_ref, i) for i in range(2)]
    u_all = [jnp.where(even, beyond[1], chip[1])] + u + [jnp.where(even, chip[0], beyond[0])]
    w_all = [jnp.where(even, beyond[0], chip[0])] + w + [jnp.where(even, chip[1], beyond[1])]
    pieces = [None] * fields
    for y in range(rows_y):
        half = (half_ref[y, k : k + 1] for k in range(3))
        hx, hy, hz = half
        pieces[y] = hy * (w_all[y + 2] - w_all[y]) - hz * diff_z(v[y])
        pieces[rows_y + y] = hz * diff_z(u[y]) - hx * diff_x(2, y)
        pieces[2 * rows_y + y] = hx * diff_x(1, y) - hy * (u_all[y + 2] - u_all[y])
    for f, piece in enumerate(pieces):
        for i, part in enumerate(split3(piece)):
            parts_ref[i * total : (i + 1) * total, f * lanes : (f + 1) * lanes] = part

    count = ref_pos_ref.shape[0]
    hot = lax.broadcasted_iota(jnp.int32, (count, fields * lanes), 1) == ref_pos_ref[...]
    hot = hot.astype(jnp.float32).astype(BF16)

    def against(rows, part):
        streamed = jnp.concatenate([hot, parts_ref[:rows]], axis=0)
        result = dot(streamed, parts_ref[part * total : (part + 1) * total], True)
        return result[:count], result[count:]

    picked_high, high = against(3 * total, 0)
    picked_middle, middle = against(2 * total, 1)
    picked_low, low = against(total, 2)
    picked = picked_low + picked_middle + picked_high
    gram = low + middle[total:] + high[2 * total :]
    gram = gram + (middle[:total] + high[total : 2 * total]) + high[:total]
    row = lax.broadcasted_iota(jnp.int32, gram.shape, 0)
    col = lax.broadcasted_iota(jnp.int32, gram.shape, 1)
    diagonal = jnp.sum(jnp.where(row == col, gram, 0.0), axis=0, keepdims=True)
    blank = jnp.zeros((lanes - count - 8, total), jnp.float32)
    extra = jnp.concatenate([picked, jnp.broadcast_to(diagonal, (8, total)), blank], axis=0).T
    h = total // 2
    row_h = lax.broadcasted_iota(jnp.int32, (h, h), 0)
    col_h = lax.broadcasted_iota(jnp.int32, (h, h), 1)
    mixed = jnp.where(row_h <= col_h, gram[:h, :h], gram[h:, h:])
    out_ref[: groups // 2, :8] = mixed.reshape(groups // 2, snaps, h)
    out_ref[groups // 2 :, :8] = gram[:h, h:].reshape(groups // 2, snaps, h)
    out_ref[:, 8:] = extra.reshape(groups, snaps, h) + leaf_ref[...][None]


def sum_spread_kernel(parts_ref, out_ref):
    total = jnp.sum(parts_ref[...], axis=0)
    for i in range(out_ref.shape[0]):
        out_ref[i] = total


def start_kernel(parts_ref, children_ref, weights_ref, rotate_ref):
    snaps = parts_ref.shape[1] // 2
    rank, total = weights_ref.shape
    levels = rotate_ref.shape[1] // total + 1
    misc = parts_ref[:, snaps:].reshape(-1, parts_ref.shape[2]).T
    count = total // misc.shape[1]
    leaves = jnp.concatenate([misc[(2 + i) * rank : (3 + i) * rank] for i in range(count)], axis=1)
    tables = jnp.concatenate(split3(children_ref[...].T), axis=0)
    width = tables.shape[1]
    child = lax.broadcasted_iota(jnp.int32, (width, total), 0)
    snap = lax.broadcasted_iota(jnp.int32, (width, total), 1)
    first, span = 0, snaps
    for level in range(levels):
        chosen = (child == first + snap // span).astype(jnp.float32).astype(BF16)
        first, span = first + total // span, span * 2
        spread = dot(tables, chosen)
        size = spread.shape[0] // 3
        spread = spread[:size] + spread[size : 2 * size] + spread[2 * size :]
        if level:
            rotate_ref[:, (level - 1) * total : level * total] = spread
        else:
            weights_ref[...] = rotated(leaves, spread)


def rotated(weights, rotate_ref):
    rank = weights.shape[0]
    total = rotate_ref[:rank] * weights[:1]
    for a in range(1, rank):
        total = total + rotate_ref[a * rank : (a + 1) * rank] * weights[a : a + 1]
    return total


def tree_kernel(cells_all, table_ref, weights_ref, rotate_ref, parts_ref, out_ref):
    groups, rows_all, lanes = table_ref.shape
    snaps = rows_all // 2
    rank = weights_ref.shape[0]
    total = groups * snaps
    h = total // 2
    packed = table_ref[:, :snaps].reshape(total, lanes)
    extra = table_ref[:, snaps:].reshape(total, lanes)
    picked = extra.T[:rank]
    mixed = packed[:h]
    cross = packed[h:]
    mixed_t = mixed.T
    row = lax.broadcasted_iota(jnp.int32, (h, h), 0)
    col = lax.broadcasted_iota(jnp.int32, (h, h), 1)
    first = jnp.where(row <= col, mixed, mixed_t)
    last = jnp.where(row > col, mixed, jnp.where(row == col, extra[h:, rank : rank + 1], mixed_t))
    first = split3(first)
    last = split3(last)
    cross = split3(cross)

    def moved_by(left):
        lower = tuple(part[:, :h] for part in left)
        upper = tuple(part[:, h:] for part in left)
        begin = mm3(lower, first) + mm3(upper, cross, True)
        return jnp.concatenate([begin, mm3(lower, cross) + mm3(upper, last)], axis=1)

    row_all = lax.broadcasted_iota(jnp.int32, (total, total), 0)
    col_all = lax.broadcasted_iota(jnp.int32, (total, total), 1)
    weights = weights_ref[...]
    levels = groups.bit_length() - 1
    for level in range(levels - 1):
        span = 2 * snaps << level
        if level:
            weights = rotated(weights, rotate_ref.at[:, (level - 1) * total : level * total])
        left = split3(weights)
        same = (row_all // span == col_all // span).astype(jnp.float32).astype(BF16)
        inside = same[:h, :h]
        begin = mm3(tuple(part[:, :h] for part in left), tuple(part * inside for part in first))
        end = mm3(tuple(part[:, h:] for part in left), tuple(part * inside for part in last))
        moved = jnp.concatenate([begin, end], axis=1)
        own = jnp.sum(weights * moved, axis=0, keepdims=True)
        products = [weights[j : j + 1] * moved for j in range(rank)]
        products = jnp.concatenate(products + [jnp.broadcast_to(own, (rank, total))], axis=0)
        upper = products.astype(BF16)
        lower = (products - upper.astype(jnp.float32)).astype(BF16)
        count = products.shape[0]
        sums = dot(jnp.concatenate([upper, lower], axis=0), same)
        sums = sums[count:] + sums[:count]
        scale = (sums[rank * rank :] + 1e-06) / rank
        turned = sums[:rank] * weights[:1]
        for j in range(1, rank):
            turned = turned + sums[j * rank : (j + 1) * rank] * weights[j : j + 1]
        weights = 1.5 * weights - 0.5 * turned / scale

    weights = rotated(weights, rotate_ref.at[:, (levels - 2) * total :])
    left = split3(weights)
    small = mm3(split3(moved_by(left)), left, True)
    identity = lax.broadcasted_iota(jnp.int32, small.shape, 0) == lax.broadcasted_iota(jnp.int32, small.shape, 1)
    scale = (jnp.sum(jnp.where(identity, small, 0.0), keepdims=True) + 1e-06) / rank
    factor = jnp.where(identity, 1.5, 0.0) - 0.5 * small / scale
    turned = factor.T
    parts = split3(turned)
    weights = mm3(parts, left)
    norm_sq = jnp.sum(turned * mm3(parts, split3(small)), axis=1, keepdims=True)
    norm_sq = jnp.maximum(norm_sq, 0.0)
    value = jnp.sum(weights * picked, axis=1, keepdims=True)
    floor_value = 0.5 * jnp.sqrt(norm_sq / cells_all + 1e-06)
    sign = value / jnp.maximum(jnp.abs(value), floor_value)
    fields = out_ref.shape[0] // rank
    modes = mm3(split3(weights), tuple(parts_ref[i * total : (i + 1) * total] for i in range(3)))
    for f in range(fields):
        out_ref[pl.ds(f, rank, stride=fields), :] = modes[:, f * lanes : (f + 1) * lanes] * sign


def call(kernel, shapes, specs, *args, name, scratch=()):
    outs = jax.tree.map(lambda _: VMEM, shapes)
    return pl.pallas_call(
        kernel,
        out_shape=shapes,
        in_specs=specs,
        out_specs=outs,
        scratch_shapes=scratch,
        name=name,
        compiler_params=pltpu.CompilerParams(vmem_limit_bytes=20 * 2**20),
    )(*args)


def f32(*shape):
    return jax.ShapeDtypeStruct(shape, jnp.float32)


def exchange(value, axis):
    return lax.all_to_all(value, axis, 0, 0, tiled=True)


def child_maps(merge_rot, merge_order):
    rank = merge_rot.shape[2]
    swapped = jnp.where(merge_order[:, None, None] == 0, merge_rot, jnp.roll(merge_rot, rank, axis=1))
    children = swapped.reshape(-1, rank * rank)
    return jnp.pad(children, ((0, -children.shape[0] % 128), (0, 0)))


def local(velocity, block_id, metric, leaf_rot, merge_rot, merge_order, ref_cell):
    snaps, _, rows_y, cells_x, cells_z = velocity.shape
    rank = leaf_rot.shape[2]
    groups = lax.axis_size(SNAP)
    slabs = lax.axis_size("space")
    snap_index = lax.axis_index(SNAP)
    space_index = lax.axis_index("space")
    fields = 3 * rows_y
    total = groups * snaps
    plane = cells_x * cells_z

    per_x = fields * snaps
    packed = pl.pallas_call(
        pack_kernel,
        out_shape=jax.ShapeDtypeStruct((cells_x, per_x, cells_z), velocity.dtype),
        in_specs=[pl.BlockSpec(memory_space=pl.ANY)],
        out_specs=pl.BlockSpec(memory_space=pl.ANY),
        scratch_shapes=[
            pltpu.VMEM((fields, snaps, cells_x, cells_z), velocity.dtype),
            pltpu.VMEM((fields, cells_x * snaps, cells_z), jnp.float32),
            pltpu.VMEM((fields, cells_x, snaps, cells_z), velocity.dtype),
            pltpu.SemaphoreType.DMA((fields,)),
            pltpu.SemaphoreType.DMA((fields,)),
        ],
        name="pack",
    )(velocity)
    own = exchange(packed, SNAP)

    children = child_maps(merge_rot, merge_order)
    rows_total = rows_y * slabs
    comp_of = ref_cell // (rows_total * plane)
    row_of = ref_cell // plane % rows_total - space_index * rows_y
    x_of = ref_cell % plane // cells_z
    here = (row_of >= 0) & (row_of < rows_y) & (x_of == snap_index)
    position = jnp.where(here, (comp_of * rows_y + row_of) * cells_z + ref_cell % cells_z, -1)
    position = position[:, None]
    ids = lax.dynamic_index_in_dim(block_id, snap_index, 1, keepdims=False)
    half = 0.5 * sum(
        jnp.where(ids[:, None] == b, metric[b][None, :, None], 0.0) for b in range(metric.shape[0])
    )
    slot = jnp.arange(cells_z, dtype=jnp.int32) // rank - 2
    leaf_here = (slot == lax.axis_index("y")) & (space_index == 0)
    leaf_tile = jnp.where(leaf_here, jnp.tile(leaf_rot[0], (1, cells_z // rank)), 0.0)

    own, children, position, half, leaf_tile = lax.optimization_barrier((own, children, position, half, leaf_tile))
    inner = own[:, snaps : 5 * snaps]
    is_even = space_index % 2 == 0
    first, last = own[:, : 2 * snaps], own[:, 4 * snaps :]
    swaps = [(i, i ^ 1) for i in range(slabs)]
    chip = lax.ppermute(jnp.where(is_even, last, first), "space", swaps)
    swaps = [(i, i - 1 if i % 2 == 0 else i + 1) for i in range(1, slabs - 1)]
    beyond = lax.ppermute(jnp.where(is_even, first, last), "space", swaps)
    even = jnp.full((8, cells_z), is_even, jnp.float32)
    left = lax.ppermute(inner, SNAP, [(i, (i + 1) % groups) for i in range(groups)])
    right = lax.ppermute(inner, SNAP, [((i + 1) % groups, i) for i in range(groups)])
    field_parts, table = call(
        gram_kernel,
        (jax.ShapeDtypeStruct((3 * total, fields * cells_z), BF16), f32(groups, 2 * snaps, cells_z)),
        [VMEM] * 9,
        half,
        position,
        own,
        left,
        right,
        chip,
        beyond,
        even,
        leaf_tile,
        name="gram",
    )
    table = exchange(table, WIDE)
    table = call(sum_spread_kernel, f32(lax.axis_size("z"), 2 * snaps, cells_z), [VMEM], table, name="sum_wide")
    parts, children = lax.optimization_barrier((exchange(table, "z"), children))
    table = call(sum_spread_kernel, f32(groups, 2 * snaps, cells_z), [VMEM], parts, name="sum_z")
    table = exchange(table, WIDE)
    levels = groups.bit_length() - 1
    weights, rotate = call(
        start_kernel,
        (f32(rank, total), f32(rank * rank, (levels - 1) * total)),
        [VMEM, VMEM],
        parts,
        children,
        name="start",
    )
    modes = call(
        functools.partial(tree_kernel, fields * plane * slabs),
        f32(rank * fields, cells_z),
        [VMEM] * 4,
        table,
        weights,
        rotate,
        field_parts,
        name="tree",
    )
    return modes.reshape(rank, 3, rows_y, cells_z)


def solution(mesh):
    torus = jax.sharding.Mesh(mesh.devices.reshape(mesh.shape["space"], 4, -1), ("space", "y", "z"))
    placed = (
        P(SNAP, None, "space", None, None),
        P("space", None, None),
        P(),
        P(SNAP, None, None),
        P(),
        P(),
        P(),
    )
    return jax.shard_map(
        local, mesh=torus, in_specs=placed, out_specs=P(None, None, "space", SNAP), check_vma=False
    )
```

```python
import functools

import jax
import jax.numpy as jnp
from jax import lax
from jax.experimental import pallas as pl
from jax.experimental.pallas import tpu as pltpu
from jax.sharding import PartitionSpec as P

HIGHEST = lax.Precision.HIGHEST
VMEM = pl.BlockSpec(memory_space=pltpu.VMEM)
SNAP = ("y", "z")
WIDE = ("space", "y")


BF16 = jnp.bfloat16


def split3(value):
    high = value.astype(BF16)
    rest = value - high.astype(jnp.float32)
    middle = rest.astype(BF16)
    low = (rest - middle.astype(jnp.float32)).astype(BF16)
    return high, middle, low


def dot(left, right, transposed=False):
    dims = (((1,), (1 if transposed else 0,)), ((), ()))
    return lax.dot_general(left, right, dims, preferred_element_type=jnp.float32)


def mm3(left, right, transposed=False):
    rows = left[0].shape[0]
    high = dot(jnp.concatenate(left, axis=0), right[0], transposed)
    middle = dot(jnp.concatenate(left[:2], axis=0), right[1], transposed)
    low = dot(left[0], right[2], transposed)
    small = low + middle[rows:] + high[2 * rows :]
    return small + (middle[:rows] + high[rows : 2 * rows]) + high[:rows]


SLOTS = {(0, 0): 0, (2, 0): 1, (1, 0): 2, (1, 1): 3, (2, 1): 4, (0, 1): 5}


def pack_kernel(vel_hbm, out_hbm, vel_ref, rows_ref, out_ref, in_sems, out_sems):
    snaps, comps, rows_y, cells_x, lanes = vel_hbm.shape
    arrivals, leaving = {}, []
    for (c, y), slot in SLOTS.items():
        arrivals[slot] = pltpu.make_async_copy(vel_hbm.at[:, c, y], vel_ref.at[slot], in_sems.at[slot])
        arrivals[slot].start()
    for slot, copy in arrivals.items():
        copy.wait()
        for s in range(snaps):
            rows_ref[slot, pl.ds(s, cells_x, stride=snaps), :] = vel_ref[slot, s].astype(jnp.float32)
        out_ref[slot] = rows_ref[slot].reshape(cells_x, snaps, lanes).astype(out_ref.dtype)
        target = out_hbm.at[:, pl.ds(slot * snaps, snaps)]
        leaving.append(pltpu.make_async_copy(out_ref.at[slot], target, out_sems.at[slot]))
        leaving[-1].start()
    for copy in leaving:
        copy.wait()


def gram_kernel(
    half_ref, ref_pos_ref, own_ref, left_ref, right_ref, chip_ref, next_ref, even_ref, side_ref,
    parts_ref, out_ref, table_ref
):
    groups, per_x, lanes = own_ref.shape
    rows_y = half_ref.shape[0]
    fields = 3 * rows_y
    snaps = per_x // fields
    total = groups * snaps

    def rows(ref, slot):
        return ref[:, slot * snaps : (slot + 1) * snaps, :].astype(jnp.float32).reshape(total, lanes)

    def diff_z(field):
        return pltpu.roll(field, lanes - 1, 1) - pltpu.roll(field, 1, 1)

    def diff_x(c, y):
        slot = SLOTS[c, y] - 1
        return rows(right_ref, slot) - rows(left_ref, slot)

    u, v, w = ([rows(own_ref, SLOTS[c, y]) for y in range(rows_y)] for c in range(3))
    even = even_ref[:1] > 0
    chip = [rows(chip_ref, i) for i in range(2)]
    beyond = [rows(next_ref, i) for i in range(2)]
    u_all = [jnp.where(even, beyond[1], chip[1])] + u + [jnp.where(even, chip[0], beyond[0])]
    w_all = [jnp.where(even, beyond[0], chip[0])] + w + [jnp.where(even, chip[1], beyond[1])]
    pieces = [None] * fields
    for y in range(rows_y):
        half = (half_ref[y, k : k + 1] for k in range(3))
        hx, hy, hz = half
        pieces[y] = hy * (w_all[y + 2] - w_all[y]) - hz * diff_z(v[y])
        pieces[rows_y + y] = hz * diff_z(u[y]) - hx * diff_x(2, y)
        pieces[2 * rows_y + y] = hx * diff_x(1, y) - hy * (u_all[y + 2] - u_all[y])
    for f, piece in enumerate(pieces):
        for i, part in enumerate(split3(piece)):
            parts_ref[i * total : (i + 1) * total, f * lanes : (f + 1) * lanes] = part

    count = ref_pos_ref.shape[0]
    hot = lax.broadcasted_iota(jnp.int32, (count, fields * lanes), 1) == ref_pos_ref[...]
    hot = hot.astype(jnp.float32).astype(BF16)

    def against(rows, part):
        streamed = jnp.concatenate([hot, parts_ref[:rows]], axis=0)
        result = dot(streamed, parts_ref[part * total : (part + 1) * total], True)
        return result[:count], result[count:]

    picked_high, high = against(3 * total, 0)
    picked_middle, middle = against(2 * total, 1)
    picked_low, low = against(total, 2)
    picked = picked_low + picked_middle + picked_high
    gram = low + middle[total:] + high[2 * total :]
    gram = gram + (middle[:total] + high[total : 2 * total]) + high[:total]
    h = total // 2
    row = lax.broadcasted_iota(jnp.int32, (h, h), 0)
    col = lax.broadcasted_iota(jnp.int32, (h, h), 1)
    last = gram[h:, h:]
    diagonal = jnp.sum(jnp.where(row == col, last, 0.0), axis=0, keepdims=True)
    table_ref[:h] = jnp.where(row <= col, gram[:h, :h], last)
    table_ref[h:] = gram[:h, h:]
    chunk = snaps + 2
    for r in range(snaps):
        out_ref[pl.ds(r, groups, stride=chunk), :] = table_ref[pl.ds(r, groups, stride=snaps), :]
    out_ref[pl.ds(snaps, groups, stride=chunk), :] = jnp.concatenate([picked[:, :h], picked[:, h:]], axis=0)
    side = side_ref[:groups] + jnp.where(side_ref[groups:] > 0, diagonal, 0.0)
    out_ref[pl.ds(snaps + 1, groups, stride=chunk), :] = side


def sum_wide_kernel(parts_ref, origin_ref, out_ref, fold_ref):
    copies, rows, lanes = out_ref.shape
    sources = 32
    chunk = parts_ref.shape[0] // sources
    block = 4 * chunk
    total = parts_ref[:block]
    for i in range(1, sources // 4):
        total = total + parts_ref[i * block : (i + 1) * block]
    fold_ref[...] = total
    total = sum(fold_ref[i * chunk : (i + 1) * chunk] for i in range(4))
    side = parts_ref[pl.ds(chunk - 1, sources, stride=chunk), :]
    origin = origin_ref[:1] > 0
    leaves = jnp.where(origin, side[4:8], side[:4])
    row = lax.broadcasted_iota(jnp.int32, side.shape, 0)
    second = (row >= 4) & (row < 8)
    diagonal = jnp.where(second, 0.0, side), jnp.where(second, side, 0.0)
    diagonal = [jnp.sum(value, axis=0, keepdims=True) for value in diagonal]
    out_ref[0, : chunk - 1] = total[: chunk - 1]
    out_ref[0, chunk - 1 : chunk] = jnp.where(origin, diagonal[0], diagonal[1])
    out_ref[0, chunk : chunk + 4] = leaves
    out_ref[0, chunk + 4 :] = jnp.zeros((rows - chunk - 4, lanes), jnp.float32)
    whole = out_ref[0]
    for i in range(1, copies):
        out_ref[i] = whole


def sum_z_kernel(parts_ref, out_ref, fold_ref):
    block = fold_ref.shape[0]
    chunk = block // 4
    total = jnp.sum(parts_ref[...], axis=0)[:chunk]
    for i in range(4):
        fold_ref[i * chunk : (i + 1) * chunk] = total
    whole = fold_ref[...]
    for i in range(out_ref.shape[0] // block):
        out_ref[i * block : (i + 1) * block] = whole


def start_kernel(parts_ref, children_ref, weights_ref, rotate_ref):
    rank, total = weights_ref.shape
    lanes = parts_ref.shape[2]
    snaps = lanes // rank
    levels = rotate_ref.shape[1] // total + 1
    leaves = jnp.concatenate([parts_ref[:, snaps + 2 + i] for i in range(4)], axis=0)
    groups = leaves.shape[0]
    own_group = lax.broadcasted_iota(jnp.int32, (groups, total), 0)
    own_group = own_group == lax.broadcasted_iota(jnp.int32, (groups, total), 1) // snaps
    wide = dot(jnp.concatenate(split3(leaves.T), axis=0), own_group.astype(jnp.float32).astype(BF16))
    wide = wide[:lanes] + wide[lanes : 2 * lanes] + wide[2 * lanes :]
    row = lax.broadcasted_iota(jnp.int32, wide.shape, 0)
    col = lax.broadcasted_iota(jnp.int32, wide.shape, 1)
    leaves = jnp.sum(jnp.where(row % snaps == col % snaps, wide, 0.0).reshape(rank, snaps, total), axis=1)
    tables = jnp.concatenate(split3(children_ref[...].T), axis=0)
    width = tables.shape[1]
    child = lax.broadcasted_iota(jnp.int32, (width, total), 0)
    snap = lax.broadcasted_iota(jnp.int32, (width, total), 1)
    first, span = 0, snaps
    for level in range(levels):
        chosen = (child == first + snap // span).astype(jnp.float32).astype(BF16)
        first, span = first + total // span, span * 2
        spread = dot(tables, chosen)
        size = spread.shape[0] // 3
        spread = spread[:size] + spread[size : 2 * size] + spread[2 * size :]
        if level:
            rotate_ref[:, (level - 1) * total : level * total] = spread
        else:
            weights_ref[...] = rotated(leaves, spread)


def rotated(weights, rotate_ref):
    rank = weights.shape[0]
    total = rotate_ref[:rank] * weights[:1]
    for a in range(1, rank):
        total = total + rotate_ref[a * rank : (a + 1) * rank] * weights[a : a + 1]
    return total


def tree_kernel(cells_all, table_ref, weights_ref, rotate_ref, parts_ref, out_ref, packed_ref):
    rank, total = weights_ref.shape
    lanes = table_ref.shape[1]
    h = total // 2
    snaps = lanes // rank
    groups = total // snaps
    chunk = snaps + 2
    for r in range(snaps):
        packed_ref[pl.ds(r, groups, stride=snaps), :] = table_ref[pl.ds(r, groups, stride=chunk), :]
    picked = table_ref[pl.ds(snaps, groups, stride=chunk), :]
    picked = jnp.concatenate([picked[:rank], picked[rank:]], axis=1)
    last_diag = table_ref[chunk - 1 : chunk] + table_ref[2 * chunk - 1 : 2 * chunk]
    mixed = packed_ref[:h]
    cross = packed_ref[h:]
    mixed_t = mixed.T
    row = lax.broadcasted_iota(jnp.int32, (h, h), 0)
    col = lax.broadcasted_iota(jnp.int32, (h, h), 1)
    first = jnp.where(row <= col, mixed, mixed_t)
    last = jnp.where(row > col, mixed, jnp.where(row == col, last_diag, mixed_t))
    first = split3(first)
    last = split3(last)
    cross = split3(cross)

    def moved_by(left):
        lower = tuple(part[:, :h] for part in left)
        upper = tuple(part[:, h:] for part in left)
        begin = mm3(lower, first) + mm3(upper, cross, True)
        return jnp.concatenate([begin, mm3(lower, cross) + mm3(upper, last)], axis=1)

    row_all = lax.broadcasted_iota(jnp.int32, (total, total), 0)
    col_all = lax.broadcasted_iota(jnp.int32, (total, total), 1)
    weights = weights_ref[...]
    levels = groups.bit_length() - 1
    for level in range(levels - 1):
        span = 2 * snaps << level
        if level:
            weights = rotated(weights, rotate_ref.at[:, (level - 1) * total : level * total])
        left = split3(weights)
        same = (row_all // span == col_all // span).astype(jnp.float32).astype(BF16)
        inside = same[:h, :h]
        begin = mm3(tuple(part[:, :h] for part in left), tuple(part * inside for part in first))
        end = mm3(tuple(part[:, h:] for part in left), tuple(part * inside for part in last))
        moved = jnp.concatenate([begin, end], axis=1)
        own = jnp.sum(weights * moved, axis=0, keepdims=True)
        products = [weights[j : j + 1] * moved for j in range(rank)]
        products = jnp.concatenate(products + [jnp.broadcast_to(own, (rank, total))], axis=0)
        upper = products.astype(BF16)
        lower = (products - upper.astype(jnp.float32)).astype(BF16)
        count = products.shape[0]
        sums = dot(jnp.concatenate([upper, lower], axis=0), same)
        sums = sums[count:] + sums[:count]
        scale = (sums[rank * rank :] + 1e-06) / rank
        turned = sums[:rank] * weights[:1]
        for j in range(1, rank):
            turned = turned + sums[j * rank : (j + 1) * rank] * weights[j : j + 1]
        weights = 1.5 * weights - 0.5 * turned / scale

    weights = rotated(weights, rotate_ref.at[:, (levels - 2) * total :])
    left = split3(weights)
    small = mm3(left, split3(moved_by(left)), True)
    small_parts = split3(small)
    turned = mm3(small_parts, left)
    identity = lax.broadcasted_iota(jnp.int32, small.shape, 0) == lax.broadcasted_iota(jnp.int32, small.shape, 1)
    scale = (jnp.sum(jnp.where(identity, small, 0.0), keepdims=True) + 1e-06) / rank
    weights = 1.5 * weights - 0.5 * turned / scale
    factor = jnp.where(identity, 1.5, 0.0) - 0.5 * small / scale
    norm_sq = jnp.sum(factor * mm3(split3(factor), small_parts), axis=1, keepdims=True)
    norm_sq = jnp.maximum(norm_sq, 0.0)
    value = jnp.sum(weights * picked, axis=1, keepdims=True)
    floor_value = 0.5 * jnp.sqrt(norm_sq / cells_all + 1e-06)
    sign = value / jnp.maximum(jnp.abs(value), floor_value)
    fields = out_ref.shape[0] // rank
    modes = mm3(split3(weights), tuple(parts_ref[i * total : (i + 1) * total] for i in range(3)))
    for f in range(fields):
        out_ref[pl.ds(f, rank, stride=fields), :] = modes[:, f * lanes : (f + 1) * lanes] * sign


def call(kernel, shapes, specs, *args, name, scratch=()):
    outs = jax.tree.map(lambda _: VMEM, shapes)
    return pl.pallas_call(
        kernel,
        out_shape=shapes,
        in_specs=specs,
        out_specs=outs,
        scratch_shapes=scratch,
        name=name,
        compiler_params=pltpu.CompilerParams(vmem_limit_bytes=20 * 2**20),
    )(*args)


def f32(*shape):
    return jax.ShapeDtypeStruct(shape, jnp.float32)


def exchange(value, axis):
    return lax.all_to_all(value, axis, 0, 0, tiled=True)


def child_maps(merge_rot, merge_order):
    rank = merge_rot.shape[2]
    swapped = jnp.where(merge_order[:, None, None] == 0, merge_rot, jnp.roll(merge_rot, rank, axis=1))
    children = swapped.reshape(-1, rank * rank)
    return jnp.pad(children, ((0, -children.shape[0] % 128), (0, 0)))


def local(velocity, block_id, metric, leaf_rot, merge_rot, merge_order, ref_cell):
    snaps, _, rows_y, cells_x, cells_z = velocity.shape
    rank = leaf_rot.shape[2]
    groups = lax.axis_size(SNAP)
    slabs = lax.axis_size("space")
    snap_index = lax.axis_index(SNAP)
    space_index = lax.axis_index("space")
    fields = 3 * rows_y
    total = groups * snaps
    plane = cells_x * cells_z

    per_x = fields * snaps
    packed = pl.pallas_call(
        pack_kernel,
        out_shape=jax.ShapeDtypeStruct((cells_x, per_x, cells_z), velocity.dtype),
        in_specs=[pl.BlockSpec(memory_space=pl.ANY)],
        out_specs=pl.BlockSpec(memory_space=pl.ANY),
        scratch_shapes=[
            pltpu.VMEM((fields, snaps, cells_x, cells_z), velocity.dtype),
            pltpu.VMEM((fields, cells_x * snaps, cells_z), jnp.float32),
            pltpu.VMEM((fields, cells_x, snaps, cells_z), velocity.dtype),
            pltpu.SemaphoreType.DMA((fields,)),
            pltpu.SemaphoreType.DMA((fields,)),
        ],
        name="pack",
    )(velocity)
    own = exchange(packed, SNAP)

    children = child_maps(merge_rot, merge_order)
    rows_total = rows_y * slabs
    comp_of = ref_cell // (rows_total * plane)
    row_of = ref_cell // plane % rows_total - space_index * rows_y
    x_of = ref_cell % plane // cells_z
    here = (row_of >= 0) & (row_of < rows_y) & (x_of == snap_index)
    position = jnp.where(here, (comp_of * rows_y + row_of) * cells_z + ref_cell % cells_z, -1)
    position = position[:, None]
    ids = lax.dynamic_index_in_dim(block_id, snap_index, 1, keepdims=False)
    half = 0.5 * sum(
        jnp.where(ids[:, None] == b, metric[b][None, :, None], 0.0) for b in range(metric.shape[0])
    )
    at = jnp.arange(groups, dtype=jnp.int32)[:, None]
    origin = (space_index == 0) & (lax.axis_index("y") == 0)
    leaf_here = ((space_index == 0) & (at != 0)) | ((space_index == 1) & (at == 0))
    diagonal_here = ((space_index != 1) & (at == 0)) | ((space_index == 1) & (at == 1))
    leaf = leaf_rot[0].T.reshape(1, cells_z)
    marks = jnp.broadcast_to(diagonal_here.astype(jnp.float32), (groups, cells_z))
    side = jnp.concatenate([jnp.where(leaf_here, leaf, 0.0), marks], axis=0)
    origin = jnp.full((8, cells_z), origin, jnp.float32)
    own, children, position, half, side, origin = lax.optimization_barrier(
        (own, children, position, half, side, origin)
    )
    inner = own[:, snaps : 5 * snaps]
    is_even = space_index % 2 == 0
    first, last = own[:, : 2 * snaps], own[:, 4 * snaps :]
    swaps = [(i, i ^ 1) for i in range(slabs)]
    chip = lax.ppermute(jnp.where(is_even, last, first), "space", swaps)
    swaps = [(i, i - 1 if i % 2 == 0 else i + 1) for i in range(1, slabs - 1)]
    beyond = lax.ppermute(jnp.where(is_even, first, last), "space", swaps)
    even = jnp.full((8, cells_z), is_even, jnp.float32)
    left = lax.ppermute(inner, SNAP, [(i, (i + 1) % groups) for i in range(groups)])
    right = lax.ppermute(inner, SNAP, [((i + 1) % groups, i) for i in range(groups)])
    chunk = snaps + 2
    field_parts, table = call(
        gram_kernel,
        (jax.ShapeDtypeStruct((3 * total, fields * cells_z), BF16), f32(groups * chunk, cells_z)),
        [VMEM] * 9,
        half,
        position,
        own,
        left,
        right,
        chip,
        beyond,
        even,
        side,
        name="gram",
        scratch=[pltpu.VMEM((total, cells_z), jnp.float32)],
    )
    fold = [pltpu.VMEM((4 * chunk, cells_z), jnp.float32)]
    pieces = (groups, chunk // 2, 2, cells_z)
    table = exchange(table.reshape(pieces), WIDE).reshape(-1, cells_z)
    depth = lax.axis_size("z")
    table = call(
        sum_wide_kernel, f32(depth, 2 * snaps, cells_z), [VMEM] * 2, table, origin, name="sum_wide", scratch=fold
    )
    parts, children = lax.optimization_barrier((exchange(table, "z"), children))
    table = call(sum_z_kernel, f32(groups * chunk, cells_z), [VMEM], parts, name="sum_z", scratch=fold)
    table = exchange(table.reshape(pieces), WIDE).reshape(-1, cells_z)
    levels = groups.bit_length() - 1
    weights, rotate = call(
        start_kernel,
        (f32(rank, total), f32(rank * rank, (levels - 1) * total)),
        [VMEM, VMEM],
        parts,
        children,
        name="start",
    )
    modes = call(
        functools.partial(tree_kernel, fields * plane * slabs),
        f32(rank * fields, cells_z),
        [VMEM] * 4,
        table,
        weights,
        rotate,
        field_parts,
        name="tree",
        scratch=[pltpu.VMEM((total, cells_z), jnp.float32)],
    )
    return modes.reshape(rank, 3, rows_y, cells_z)


def solution(mesh):
    torus = jax.sharding.Mesh(mesh.devices.reshape(mesh.shape["space"], 4, -1), ("space", "y", "z"))
    placed = (
        P(SNAP, None, "space", None, None),
        P("space", None, None),
        P(),
        P(SNAP, None, None),
        P(),
        P(),
        P(),
    )
    return jax.shard_map(
        local, mesh=torus, in_specs=placed, out_specs=P(None, None, "space", SNAP), check_vma=False
    )
```

```python
import functools

import jax
import jax.numpy as jnp
from jax import lax
from jax.experimental import pallas as pl
from jax.experimental.pallas import tpu as pltpu
from jax.sharding import PartitionSpec as P

HIGHEST = lax.Precision.HIGHEST
VMEM = pl.BlockSpec(memory_space=pltpu.VMEM)
SNAP = ("y", "z")
WIDE = ("space", "y")


BF16 = jnp.bfloat16


def split3(value):
    high = value.astype(BF16)
    rest = value - high.astype(jnp.float32)
    middle = rest.astype(BF16)
    low = (rest - middle.astype(jnp.float32)).astype(BF16)
    return high, middle, low


def dot(left, right, transposed=False):
    dims = (((1,), (1 if transposed else 0,)), ((), ()))
    return lax.dot_general(left, right, dims, preferred_element_type=jnp.float32)


def mm3(left, right, transposed=False):
    rows = left[0].shape[0]
    high = dot(jnp.concatenate(left, axis=0), right[0], transposed)
    middle = dot(jnp.concatenate(left[:2], axis=0), right[1], transposed)
    low = dot(left[0], right[2], transposed)
    small = low + middle[rows:] + high[2 * rows :]
    return small + (middle[:rows] + high[rows : 2 * rows]) + high[:rows]


SLOTS = {(0, 0): 0, (2, 0): 1, (1, 0): 2, (1, 1): 3, (2, 1): 4, (0, 1): 5}


def pack_kernel(vel_hbm, out_hbm, vel_ref, rows_ref, out_ref, in_sems, out_sems):
    snaps, comps, rows_y, cells_x, lanes = vel_hbm.shape
    arrivals, leaving = {}, []
    for (c, y), slot in SLOTS.items():
        arrivals[slot] = pltpu.make_async_copy(vel_hbm.at[:, c, y], vel_ref.at[slot], in_sems.at[slot])
        arrivals[slot].start()
    for slot, copy in arrivals.items():
        copy.wait()
        for s in range(snaps):
            rows_ref[slot, pl.ds(s, cells_x, stride=snaps), :] = vel_ref[slot, s].astype(jnp.float32)
        out_ref[slot] = rows_ref[slot].reshape(cells_x, snaps, lanes).astype(out_ref.dtype)
        target = out_hbm.at[:, pl.ds(slot * snaps, snaps)]
        leaving.append(pltpu.make_async_copy(out_ref.at[slot], target, out_sems.at[slot]))
        leaving[-1].start()
    for copy in leaving:
        copy.wait()


def gram_kernel(
    half_ref, ref_pos_ref, own_ref, left_ref, right_ref, chip_ref, next_ref, even_ref, side_ref,
    parts_ref, out_ref, table_ref
):
    groups, per_x, lanes = own_ref.shape
    rows_y = half_ref.shape[0]
    fields = 3 * rows_y
    snaps = per_x // fields
    total = groups * snaps

    def rows(ref, slot):
        return ref[:, slot * snaps : (slot + 1) * snaps, :].astype(jnp.float32).reshape(total, lanes)

    def diff_z(field):
        return pltpu.roll(field, lanes - 1, 1) - pltpu.roll(field, 1, 1)

    def diff_x(c, y):
        slot = SLOTS[c, y] - 1
        return rows(right_ref, slot) - rows(left_ref, slot)

    u, v, w = ([rows(own_ref, SLOTS[c, y]) for y in range(rows_y)] for c in range(3))
    even = even_ref[:1] > 0
    chip = [rows(chip_ref, i) for i in range(2)]
    beyond = [rows(next_ref, i) for i in range(2)]
    u_all = [jnp.where(even, beyond[1], chip[1])] + u + [jnp.where(even, chip[0], beyond[0])]
    w_all = [jnp.where(even, beyond[0], chip[0])] + w + [jnp.where(even, chip[1], beyond[1])]
    pieces = [None] * fields
    for y in range(rows_y):
        half = (half_ref[y, k : k + 1] for k in range(3))
        hx, hy, hz = half
        pieces[y] = hy * (w_all[y + 2] - w_all[y]) - hz * diff_z(v[y])
        pieces[rows_y + y] = hz * diff_z(u[y]) - hx * diff_x(2, y)
        pieces[2 * rows_y + y] = hx * diff_x(1, y) - hy * (u_all[y + 2] - u_all[y])
    for f, piece in enumerate(pieces):
        for i, part in enumerate(split3(piece)):
            parts_ref[i * total : (i + 1) * total, f * lanes : (f + 1) * lanes] = part

    count = ref_pos_ref.shape[0]
    hot = lax.broadcasted_iota(jnp.int32, (count, fields * lanes), 1) == ref_pos_ref[...]
    hot = hot.astype(jnp.float32).astype(BF16)

    def against(rows, part):
        streamed = jnp.concatenate([hot, parts_ref[:rows]], axis=0)
        result = dot(streamed, parts_ref[part * total : (part + 1) * total], True)
        return result[:count], result[count:]

    picked_high, high = against(3 * total, 0)
    picked_middle, middle = against(2 * total, 1)
    picked_low, low = against(total, 2)
    picked = picked_low + picked_middle + picked_high
    gram = low + middle[total:] + high[2 * total :]
    gram = gram + (middle[:total] + high[total : 2 * total]) + high[:total]
    h = total // 2
    row = lax.broadcasted_iota(jnp.int32, (h, h), 0)
    col = lax.broadcasted_iota(jnp.int32, (h, h), 1)
    last = gram[h:, h:]
    diagonal = jnp.sum(jnp.where(row == col, last, 0.0), axis=0, keepdims=True)
    table_ref[:h] = jnp.where(row <= col, gram[:h, :h], last)
    table_ref[h:] = gram[:h, h:]
    chunk = snaps + 2
    for r in range(snaps):
        out_ref[pl.ds(r, groups, stride=chunk), :] = table_ref[pl.ds(r, groups, stride=snaps), :]
    out_ref[pl.ds(snaps, groups, stride=chunk), :] = jnp.concatenate([picked[:, :h], picked[:, h:]], axis=0)
    side = side_ref[:groups] + jnp.where(side_ref[groups:] > 0, diagonal, 0.0)
    out_ref[pl.ds(snaps + 1, groups, stride=chunk), :] = side


def sum_wide_kernel(parts_ref, origin_ref, out_ref, fold_ref):
    copies, rows, lanes = out_ref.shape
    sources = 32
    chunk = parts_ref.shape[0] // sources
    block = 4 * chunk
    total = parts_ref[:block]
    for i in range(1, sources // 4):
        total = total + parts_ref[i * block : (i + 1) * block]
    fold_ref[...] = total
    total = sum(fold_ref[i * chunk : (i + 1) * chunk] for i in range(4))
    side = parts_ref[pl.ds(chunk - 1, sources, stride=chunk), :]
    origin = origin_ref[:1] > 0
    leaves = jnp.where(origin, side[4:8], side[:4])
    row = lax.broadcasted_iota(jnp.int32, side.shape, 0)
    second = (row >= 4) & (row < 8)
    diagonal = jnp.where(second, 0.0, side), jnp.where(second, side, 0.0)
    diagonal = [jnp.sum(value, axis=0, keepdims=True) for value in diagonal]
    out_ref[0, : chunk - 1] = total[: chunk - 1]
    out_ref[0, chunk - 1 : chunk] = jnp.where(origin, diagonal[0], diagonal[1])
    out_ref[0, chunk : chunk + 4] = leaves
    out_ref[0, chunk + 4 :] = jnp.zeros((rows - chunk - 4, lanes), jnp.float32)
    whole = out_ref[0]
    for i in range(1, copies):
        out_ref[i] = whole


def sum_z_kernel(parts_ref, out_ref, fold_ref):
    block = fold_ref.shape[0]
    chunk = block // 4
    total = jnp.sum(parts_ref[...], axis=0)[:chunk]
    for i in range(4):
        fold_ref[i * chunk : (i + 1) * chunk] = total
    whole = fold_ref[...]
    for i in range(out_ref.shape[0] // block):
        out_ref[i * block : (i + 1) * block] = whole


def tables_kernel(children_ref, rest_hbm, rest_ref, sems):
    count, size, total = rest_hbm.shape
    tables = jnp.concatenate(split3(children_ref[...].T), axis=0)
    width = tables.shape[1]
    child = lax.broadcasted_iota(jnp.int32, (width, total), 0)
    snap = lax.broadcasted_iota(jnp.int32, (width, total), 1)
    span = total >> count
    first = 2 * (total // span)
    copies = []
    for level in range(count):
        chosen = (child == first + snap // span).astype(jnp.float32).astype(BF16)
        first, span = first + total // span, span * 2
        spread = dot(tables, chosen)
        rest_ref[level] = spread[:size] + spread[size : 2 * size] + spread[2 * size :]
        copies.append(pltpu.make_async_copy(rest_ref.at[level], rest_hbm.at[level], sems.at[level]))
        copies[-1].start()
    for copy in copies:
        copy.wait()


def leaf_weights(pieces_ref, rank, total):
    lanes = pieces_ref.shape[2]
    snaps = lanes // rank
    leaves = jnp.concatenate([pieces_ref[:, snaps + 2 + i] for i in range(4)], axis=0)
    groups = leaves.shape[0]
    own_group = lax.broadcasted_iota(jnp.int32, (groups, total), 0)
    own_group = own_group == lax.broadcasted_iota(jnp.int32, (groups, total), 1) // snaps
    wide = dot(jnp.concatenate(split3(leaves.T), axis=0), own_group.astype(jnp.float32).astype(BF16))
    wide = wide[:lanes] + wide[lanes : 2 * lanes] + wide[2 * lanes :]
    row = lax.broadcasted_iota(jnp.int32, wide.shape, 0)
    col = lax.broadcasted_iota(jnp.int32, wide.shape, 1)
    return jnp.sum(jnp.where(row % snaps == col % snaps, wide, 0.0).reshape(rank, snaps, total), axis=1)


def rotated(weights, rotate_ref):
    rank = weights.shape[0]
    total = rotate_ref[:rank] * weights[:1]
    for a in range(1, rank):
        total = total + rotate_ref[a * rank : (a + 1) * rank] * weights[a : a + 1]
    return total


def tree_kernel(
    cells_all, table_ref, pieces_ref, rest_ref, parts_ref, out_ref, packed_ref
):
    total = rest_ref.shape[2]
    lanes = table_ref.shape[1]
    rank = out_ref.shape[0] * lanes // parts_ref.shape[1]
    h = total // 2
    snaps = lanes // rank
    groups = total // snaps
    chunk = snaps + 2
    for r in range(snaps):
        packed_ref[pl.ds(r, groups, stride=snaps), :] = table_ref[pl.ds(r, groups, stride=chunk), :]
    picked = table_ref[pl.ds(snaps, groups, stride=chunk), :]
    picked = jnp.concatenate([picked[:rank], picked[rank:]], axis=1)
    last_diag = table_ref[chunk - 1 : chunk] + table_ref[2 * chunk - 1 : 2 * chunk]
    mixed = packed_ref[:h]
    cross = packed_ref[h:]
    mixed_t = mixed.T
    row = lax.broadcasted_iota(jnp.int32, (h, h), 0)
    col = lax.broadcasted_iota(jnp.int32, (h, h), 1)
    first = jnp.where(row <= col, mixed, mixed_t)
    last = jnp.where(row > col, mixed, jnp.where(row == col, last_diag, mixed_t))
    first = split3(first)
    last = split3(last)
    cross = split3(cross)

    def moved_by(left):
        lower = tuple(part[:, :h] for part in left)
        upper = tuple(part[:, h:] for part in left)
        begin = mm3(lower, first) + mm3(upper, cross, True)
        return jnp.concatenate([begin, mm3(lower, cross) + mm3(upper, last)], axis=1)

    row_all = lax.broadcasted_iota(jnp.int32, (total, total), 0)
    col_all = lax.broadcasted_iota(jnp.int32, (total, total), 1)
    weights = leaf_weights(pieces_ref, rank, total)
    levels = groups.bit_length() - 1
    for level in range(levels - 1):
        span = 2 * snaps << level
        if level:
            weights = rotated(weights, rest_ref.at[level - 1])
        left = split3(weights)
        same = (row_all // span == col_all // span).astype(jnp.float32).astype(BF16)
        inside = same[:h, :h]
        begin = mm3(tuple(part[:, :h] for part in left), tuple(part * inside for part in first))
        end = mm3(tuple(part[:, h:] for part in left), tuple(part * inside for part in last))
        moved = jnp.concatenate([begin, end], axis=1)
        own = jnp.sum(weights * moved, axis=0, keepdims=True)
        products = [weights[j : j + 1] * moved for j in range(rank)]
        products = jnp.concatenate(products + [jnp.broadcast_to(own, (rank, total))], axis=0)
        upper = products.astype(BF16)
        lower = (products - upper.astype(jnp.float32)).astype(BF16)
        count = products.shape[0]
        sums = dot(jnp.concatenate([upper, lower], axis=0), same)
        sums = sums[count:] + sums[:count]
        scale = (sums[rank * rank :] + 1e-06) / rank
        turned = sums[:rank] * weights[:1]
        for j in range(1, rank):
            turned = turned + sums[j * rank : (j + 1) * rank] * weights[j : j + 1]
        weights = 1.5 * weights - 0.5 * turned / scale

    weights = rotated(weights, rest_ref.at[levels - 2])
    left = split3(weights)
    small = mm3(left, split3(moved_by(left)), True)
    small_parts = split3(small)
    turned = mm3(small_parts, left)
    identity = lax.broadcasted_iota(jnp.int32, small.shape, 0) == lax.broadcasted_iota(jnp.int32, small.shape, 1)
    scale = (jnp.sum(jnp.where(identity, small, 0.0), keepdims=True) + 1e-06) / rank
    weights = 1.5 * weights - 0.5 * turned / scale
    factor = jnp.where(identity, 1.5, 0.0) - 0.5 * small / scale
    norm_sq = jnp.sum(factor * mm3(split3(factor), small_parts), axis=1, keepdims=True)
    norm_sq = jnp.maximum(norm_sq, 0.0)
    value = jnp.sum(weights * picked, axis=1, keepdims=True)
    floor_value = 0.5 * jnp.sqrt(norm_sq / cells_all + 1e-06)
    sign = value / jnp.maximum(jnp.abs(value), floor_value)
    fields = out_ref.shape[0] // rank
    modes = mm3(split3(weights), tuple(parts_ref[i * total : (i + 1) * total] for i in range(3)))
    for f in range(fields):
        out_ref[pl.ds(f, rank, stride=fields), :] = modes[:, f * lanes : (f + 1) * lanes] * sign


def call(kernel, shapes, specs, *args, name, scratch=()):
    outs = jax.tree.map(lambda _: VMEM, shapes)
    return pl.pallas_call(
        kernel,
        out_shape=shapes,
        in_specs=specs,
        out_specs=outs,
        scratch_shapes=scratch,
        name=name,
        compiler_params=pltpu.CompilerParams(vmem_limit_bytes=20 * 2**20),
    )(*args)


def f32(*shape):
    return jax.ShapeDtypeStruct(shape, jnp.float32)


def exchange(value, axis):
    return lax.all_to_all(value, axis, 0, 0, tiled=True)


def child_maps(merge_rot, merge_order):
    rank = merge_rot.shape[2]
    swapped = jnp.where(merge_order[:, None, None] == 0, merge_rot, jnp.roll(merge_rot, rank, axis=1))
    children = swapped.reshape(-1, rank * rank)
    return jnp.pad(children, ((0, -children.shape[0] % 128), (0, 0)))


def local(velocity, block_id, metric, leaf_rot, merge_rot, merge_order, ref_cell):
    snaps, _, rows_y, cells_x, cells_z = velocity.shape
    rank = leaf_rot.shape[2]
    groups = lax.axis_size(SNAP)
    slabs = lax.axis_size("space")
    snap_index = lax.axis_index(SNAP)
    space_index = lax.axis_index("space")
    fields = 3 * rows_y
    total = groups * snaps
    plane = cells_x * cells_z

    per_x = fields * snaps
    packed = pl.pallas_call(
        pack_kernel,
        out_shape=jax.ShapeDtypeStruct((cells_x, per_x, cells_z), velocity.dtype),
        in_specs=[pl.BlockSpec(memory_space=pl.ANY)],
        out_specs=pl.BlockSpec(memory_space=pl.ANY),
        scratch_shapes=[
            pltpu.VMEM((fields, snaps, cells_x, cells_z), velocity.dtype),
            pltpu.VMEM((fields, cells_x * snaps, cells_z), jnp.float32),
            pltpu.VMEM((fields, cells_x, snaps, cells_z), velocity.dtype),
            pltpu.SemaphoreType.DMA((fields,)),
            pltpu.SemaphoreType.DMA((fields,)),
        ],
        name="pack",
    )(velocity)
    own = exchange(packed, SNAP)

    levels = groups.bit_length() - 1
    rest_shape = (levels - 1, rank * rank, total)
    children = child_maps(merge_rot, merge_order)
    rest = pl.pallas_call(
        tables_kernel,
        out_shape=f32(*rest_shape),
        in_specs=[VMEM],
        out_specs=pl.BlockSpec(memory_space=pltpu.HBM),
        scratch_shapes=[pltpu.VMEM(rest_shape, jnp.float32), pltpu.SemaphoreType.DMA((levels - 1,))],
        name="tables",
    )(children)
    own_map = lax.dynamic_index_in_dim(children, snap_index, 0, keepdims=False).reshape(rank, rank)
    leaf = jnp.sum(own_map[:, :, None] * leaf_rot[0].T[:, None, :], axis=0).reshape(1, cells_z)
    rows_total = rows_y * slabs
    comp_of = ref_cell // (rows_total * plane)
    row_of = ref_cell // plane % rows_total - space_index * rows_y
    x_of = ref_cell % plane // cells_z
    here = (row_of >= 0) & (row_of < rows_y) & (x_of == snap_index)
    position = jnp.where(here, (comp_of * rows_y + row_of) * cells_z + ref_cell % cells_z, -1)
    position = position[:, None]
    ids = lax.dynamic_index_in_dim(block_id, snap_index, 1, keepdims=False)
    half = 0.5 * sum(
        jnp.where(ids[:, None] == b, metric[b][None, :, None], 0.0) for b in range(metric.shape[0])
    )
    at = jnp.arange(groups, dtype=jnp.int32)[:, None]
    origin = (space_index == 0) & (lax.axis_index("y") == 0)
    leaf_here = ((space_index == 0) & (at != 0)) | ((space_index == 1) & (at == 0))
    diagonal_here = ((space_index != 1) & (at == 0)) | ((space_index == 1) & (at == 1))
    marks = jnp.broadcast_to(diagonal_here.astype(jnp.float32), (groups, cells_z))
    side = jnp.concatenate([jnp.where(leaf_here, leaf, 0.0), marks], axis=0)
    origin = jnp.full((8, cells_z), origin, jnp.float32)
    own, rest, position, half, side, origin = lax.optimization_barrier((own, rest, position, half, side, origin))
    inner = own[:, snaps : 5 * snaps]
    is_even = space_index % 2 == 0
    low, high = own[:, : 2 * snaps], own[:, 4 * snaps :]
    swaps = [(i, i ^ 1) for i in range(slabs)]
    chip = lax.ppermute(jnp.where(is_even, high, low), "space", swaps)
    swaps = [(i, i - 1 if i % 2 == 0 else i + 1) for i in range(1, slabs - 1)]
    beyond = lax.ppermute(jnp.where(is_even, low, high), "space", swaps)
    even = jnp.full((8, cells_z), is_even, jnp.float32)
    left = lax.ppermute(inner, SNAP, [(i, (i + 1) % groups) for i in range(groups)])
    right = lax.ppermute(inner, SNAP, [((i + 1) % groups, i) for i in range(groups)])
    chunk = snaps + 2
    field_parts, table = call(
        gram_kernel,
        (jax.ShapeDtypeStruct((3 * total, fields * cells_z), BF16), f32(groups * chunk, cells_z)),
        [VMEM] * 9,
        half,
        position,
        own,
        left,
        right,
        chip,
        beyond,
        even,
        side,
        name="gram",
        scratch=[pltpu.VMEM((total, cells_z), jnp.float32)],
    )
    fold = [pltpu.VMEM((4 * chunk, cells_z), jnp.float32)]
    pieces = (groups, chunk // 2, 2, cells_z)
    table = exchange(table.reshape(pieces), WIDE).reshape(-1, cells_z)
    depth = lax.axis_size("z")
    table = call(
        sum_wide_kernel, f32(depth, 2 * snaps, cells_z), [VMEM] * 2, table, origin, name="sum_wide", scratch=fold
    )
    parts = exchange(table, "z")
    table = call(sum_z_kernel, f32(groups * chunk, cells_z), [VMEM], parts, name="sum_z", scratch=fold)
    table = exchange(table.reshape(pieces), WIDE).reshape(-1, cells_z)
    modes = call(
        functools.partial(tree_kernel, fields * plane * slabs),
        f32(rank * fields, cells_z),
        [VMEM] * 4,
        table,
        parts,
        rest,
        field_parts,
        name="tree",
        scratch=[pltpu.VMEM((total, cells_z), jnp.float32)],
    )
    return modes.reshape(rank, 3, rows_y, cells_z)


def solution(mesh):
    torus = jax.sharding.Mesh(mesh.devices.reshape(mesh.shape["space"], 4, -1), ("space", "y", "z"))
    placed = (
        P(SNAP, None, "space", None, None),
        P("space", None, None),
        P(),
        P(SNAP, None, None),
        P(),
        P(),
        P(),
    )
    return jax.shard_map(
        local, mesh=torus, in_specs=placed, out_specs=P(None, None, "space", SNAP), check_vma=False
    )
```

```python
import functools

import jax
import jax.numpy as jnp
from jax import lax
from jax.experimental import pallas as pl
from jax.experimental.pallas import tpu as pltpu
from jax.sharding import PartitionSpec as P

HIGHEST = lax.Precision.HIGHEST
VMEM = pl.BlockSpec(memory_space=pltpu.VMEM)
SNAP = ("y", "z")
WIDE = ("space", "y")


BF16 = jnp.bfloat16


def split3(value):
    high = value.astype(BF16)
    rest = value - high.astype(jnp.float32)
    middle = rest.astype(BF16)
    low = (rest - middle.astype(jnp.float32)).astype(BF16)
    return high, middle, low


def dot(left, right, transposed=False):
    dims = (((1,), (1 if transposed else 0,)), ((), ()))
    return lax.dot_general(left, right, dims, preferred_element_type=jnp.float32)


def mm3(left, right, transposed=False):
    rows = left[0].shape[0]
    high = dot(jnp.concatenate(left, axis=0), right[0], transposed)
    middle = dot(jnp.concatenate(left[:2], axis=0), right[1], transposed)
    low = dot(left[0], right[2], transposed)
    small = low + middle[rows:] + high[2 * rows :]
    return small + (middle[:rows] + high[rows : 2 * rows]) + high[:rows]


SLOTS = {(0, 0): 0, (2, 0): 1, (1, 0): 2, (1, 1): 3, (2, 1): 4, (0, 1): 5}


def pack_kernel(vel_hbm, out_hbm, vel_ref, rows_ref, out_ref, in_sems, out_sems):
    snaps, comps, rows_y, cells_x, lanes = vel_hbm.shape
    arrivals, leaving = {}, []
    for c in range(comps):
        arrivals[c] = pltpu.make_async_copy(vel_hbm.at[:, c], vel_ref.at[c], in_sems.at[c])
        arrivals[c].start()
    for (c, y), slot in sorted(SLOTS.items()):
        if y == 0:
            arrivals[c].wait()
        for s in range(snaps):
            rows_ref[slot, pl.ds(s, cells_x, stride=snaps), :] = vel_ref[c, s, y].astype(jnp.float32)
        out_ref[slot] = rows_ref[slot].reshape(cells_x, snaps, lanes).astype(out_ref.dtype)
        target = out_hbm.at[:, pl.ds(slot * snaps, snaps)]
        leaving.append(pltpu.make_async_copy(out_ref.at[slot], target, out_sems.at[slot]))
        leaving[-1].start()
    for copy in leaving:
        copy.wait()


def gram_kernel(
    half_ref, ref_pos_ref, own_ref, left_ref, right_ref, chip_ref, next_ref, even_ref, side_ref,
    parts_ref, out_ref, table_ref
):
    groups, per_x, lanes = own_ref.shape
    rows_y = half_ref.shape[0]
    fields = 3 * rows_y
    snaps = per_x // fields
    total = groups * snaps

    def rows(ref, slot):
        return ref[:, slot * snaps : (slot + 1) * snaps, :].astype(jnp.float32).reshape(total, lanes)

    def diff_z(field):
        return pltpu.roll(field, lanes - 1, 1) - pltpu.roll(field, 1, 1)

    def diff_x(c, y):
        slot = SLOTS[c, y] - 1
        return rows(right_ref, slot) - rows(left_ref, slot)

    u, v, w = ([rows(own_ref, SLOTS[c, y]) for y in range(rows_y)] for c in range(3))
    even = even_ref[:1] > 0
    chip = [rows(chip_ref, i) for i in range(2)]
    beyond = [rows(next_ref, i) for i in range(2)]
    u_all = [jnp.where(even, beyond[1], chip[1])] + u + [jnp.where(even, chip[0], beyond[0])]
    w_all = [jnp.where(even, beyond[0], chip[0])] + w + [jnp.where(even, chip[1], beyond[1])]
    pieces = [None] * fields
    for y in range(rows_y):
        half = (half_ref[y, k : k + 1] for k in range(3))
        hx, hy, hz = half
        pieces[y] = hy * (w_all[y + 2] - w_all[y]) - hz * diff_z(v[y])
        pieces[rows_y + y] = hz * diff_z(u[y]) - hx * diff_x(2, y)
        pieces[2 * rows_y + y] = hx * diff_x(1, y) - hy * (u_all[y + 2] - u_all[y])
    for f, piece in enumerate(pieces):
        for i, part in enumerate(split3(piece)):
            parts_ref[i * total : (i + 1) * total, f * lanes : (f + 1) * lanes] = part

    count = ref_pos_ref.shape[0]
    hot = lax.broadcasted_iota(jnp.int32, (count, fields * lanes), 1) == ref_pos_ref[...]
    hot = hot.astype(jnp.float32).astype(BF16)

    def against(rows, part):
        streamed = jnp.concatenate([hot, parts_ref[:rows]], axis=0)
        result = dot(streamed, parts_ref[part * total : (part + 1) * total], True)
        return result[:count], result[count:]

    picked_high, high = against(3 * total, 0)
    picked_middle, middle = against(2 * total, 1)
    picked_low, low = against(total, 2)
    picked = picked_low + picked_middle + picked_high
    gram = low + middle[total:] + high[2 * total :]
    gram = gram + (middle[:total] + high[total : 2 * total]) + high[:total]
    h = total // 2
    row = lax.broadcasted_iota(jnp.int32, (h, h), 0)
    col = lax.broadcasted_iota(jnp.int32, (h, h), 1)
    last = gram[h:, h:]
    diagonal = jnp.sum(jnp.where(row == col, last, 0.0), axis=0, keepdims=True)
    table_ref[:h] = jnp.where(row <= col, gram[:h, :h], last)
    table_ref[h:] = gram[:h, h:]
    chunk = snaps + 2
    for r in range(snaps):
        out_ref[pl.ds(r, groups, stride=chunk), :] = table_ref[pl.ds(r, groups, stride=snaps), :]
    out_ref[pl.ds(snaps, groups, stride=chunk), :] = jnp.concatenate([picked[:, :h], picked[:, h:]], axis=0)
    side = side_ref[:groups] + jnp.where(side_ref[groups:] > 0, diagonal, 0.0)
    out_ref[pl.ds(snaps + 1, groups, stride=chunk), :] = side


def sum_wide_kernel(parts_ref, origin_ref, out_ref, fold_ref):
    copies, rows, lanes = out_ref.shape
    sources = 32
    chunk = parts_ref.shape[0] // sources
    block = 4 * chunk
    total = parts_ref[:block]
    for i in range(1, sources // 4):
        total = total + parts_ref[i * block : (i + 1) * block]
    fold_ref[...] = total
    total = sum(fold_ref[i * chunk : (i + 1) * chunk] for i in range(4))
    side = parts_ref[pl.ds(chunk - 1, sources, stride=chunk), :]
    origin = origin_ref[:1] > 0
    leaves = jnp.where(origin, side[4:8], side[:4])
    row = lax.broadcasted_iota(jnp.int32, side.shape, 0)
    second = (row >= 4) & (row < 8)
    diagonal = jnp.where(second, 0.0, side), jnp.where(second, side, 0.0)
    diagonal = [jnp.sum(value, axis=0, keepdims=True) for value in diagonal]
    out_ref[0, : chunk - 1] = total[: chunk - 1]
    out_ref[0, chunk - 1 : chunk] = jnp.where(origin, diagonal[0], diagonal[1])
    out_ref[0, chunk : chunk + 4] = leaves
    out_ref[0, chunk + 4 :] = jnp.zeros((rows - chunk - 4, lanes), jnp.float32)
    whole = out_ref[0]
    for i in range(1, copies):
        out_ref[i] = whole


def sum_z_kernel(parts_ref, out_ref, fold_ref):
    block = fold_ref.shape[0]
    chunk = block // 4
    total = jnp.sum(parts_ref[...], axis=0)[:chunk]
    for i in range(4):
        fold_ref[i * chunk : (i + 1) * chunk] = total
    whole = fold_ref[...]
    for i in range(out_ref.shape[0] // block):
        out_ref[i * block : (i + 1) * block] = whole


def tables_kernel(children_ref, rest_hbm, rest_ref, sems):
    count, size, total = rest_hbm.shape
    tables = jnp.concatenate(split3(children_ref[...].T), axis=0)
    width = tables.shape[1]
    child = lax.broadcasted_iota(jnp.int32, (width, total), 0)
    snap = lax.broadcasted_iota(jnp.int32, (width, total), 1)
    span = total >> count
    first = 2 * (total // span)
    copies = []
    for level in range(count):
        chosen = (child == first + snap // span).astype(jnp.float32).astype(BF16)
        first, span = first + total // span, span * 2
        spread = dot(tables, chosen)
        rest_ref[level] = spread[:size] + spread[size : 2 * size] + spread[2 * size :]
        copies.append(pltpu.make_async_copy(rest_ref.at[level], rest_hbm.at[level], sems.at[level]))
        copies[-1].start()
    for copy in copies:
        copy.wait()


def leaf_weights(pieces_ref, rank, total):
    lanes = pieces_ref.shape[2]
    snaps = lanes // rank
    leaves = jnp.concatenate([pieces_ref[:, snaps + 2 + i] for i in range(4)], axis=0)
    groups = leaves.shape[0]
    own_group = lax.broadcasted_iota(jnp.int32, (groups, total), 0)
    own_group = own_group == lax.broadcasted_iota(jnp.int32, (groups, total), 1) // snaps
    wide = dot(jnp.concatenate(split3(leaves.T), axis=0), own_group.astype(jnp.float32).astype(BF16))
    wide = wide[:lanes] + wide[lanes : 2 * lanes] + wide[2 * lanes :]
    row = lax.broadcasted_iota(jnp.int32, wide.shape, 0)
    col = lax.broadcasted_iota(jnp.int32, wide.shape, 1)
    return jnp.sum(jnp.where(row % snaps == col % snaps, wide, 0.0).reshape(rank, snaps, total), axis=1)


def rotated(weights, rotate_ref):
    rank = weights.shape[0]
    total = rotate_ref[:rank] * weights[:1]
    for a in range(1, rank):
        total = total + rotate_ref[a * rank : (a + 1) * rank] * weights[a : a + 1]
    return total


def tree_kernel(
    cells_all, table_ref, pieces_ref, rest_ref, parts_ref, out_ref, packed_ref
):
    total = rest_ref.shape[2]
    lanes = table_ref.shape[1]
    rank = out_ref.shape[0] * lanes // parts_ref.shape[1]
    h = total // 2
    snaps = lanes // rank
    groups = total // snaps
    chunk = snaps + 2
    for r in range(snaps):
        packed_ref[pl.ds(r, groups, stride=snaps), :] = table_ref[pl.ds(r, groups, stride=chunk), :]
    picked = table_ref[pl.ds(snaps, groups, stride=chunk), :]
    picked = jnp.concatenate([picked[:rank], picked[rank:]], axis=1)
    last_diag = table_ref[chunk - 1 : chunk] + table_ref[2 * chunk - 1 : 2 * chunk]
    mixed = packed_ref[:h]
    cross = packed_ref[h:]
    mixed_t = mixed.T
    row = lax.broadcasted_iota(jnp.int32, (h, h), 0)
    col = lax.broadcasted_iota(jnp.int32, (h, h), 1)
    first = jnp.where(row <= col, mixed, mixed_t)
    last = jnp.where(row > col, mixed, jnp.where(row == col, last_diag, mixed_t))
    first = split3(first)
    last = split3(last)
    cross = split3(cross)

    def moved_by(left):
        lower = tuple(part[:, :h] for part in left)
        upper = tuple(part[:, h:] for part in left)
        begin = mm3(lower, first) + mm3(upper, cross, True)
        return jnp.concatenate([begin, mm3(lower, cross) + mm3(upper, last)], axis=1)

    row_all = lax.broadcasted_iota(jnp.int32, (total, total), 0)
    col_all = lax.broadcasted_iota(jnp.int32, (total, total), 1)
    weights = leaf_weights(pieces_ref, rank, total)
    levels = groups.bit_length() - 1
    for level in range(levels - 1):
        span = 2 * snaps << level
        if level:
            weights = rotated(weights, rest_ref.at[level - 1])
        left = split3(weights)
        same = (row_all // span == col_all // span).astype(jnp.float32).astype(BF16)
        inside = same[:h, :h]
        begin = mm3(tuple(part[:, :h] for part in left), tuple(part * inside for part in first))
        end = mm3(tuple(part[:, h:] for part in left), tuple(part * inside for part in last))
        moved = jnp.concatenate([begin, end], axis=1)
        own = jnp.sum(weights * moved, axis=0, keepdims=True)
        products = [weights[j : j + 1] * moved for j in range(rank)]
        products = jnp.concatenate(products + [jnp.broadcast_to(own, (rank, total))], axis=0)
        upper = products.astype(BF16)
        lower = (products - upper.astype(jnp.float32)).astype(BF16)
        count = products.shape[0]
        sums = dot(jnp.concatenate([upper, lower], axis=0), same)
        sums = sums[count:] + sums[:count]
        share = 0.5 * rank / (sums[rank * rank :] + 1e-06)
        turned = sums[:rank] * weights[:1]
        for j in range(1, rank):
            turned = turned + sums[j * rank : (j + 1) * rank] * weights[j : j + 1]
        weights = 1.5 * weights - turned * share

    weights = rotated(weights, rest_ref.at[levels - 2])
    left = split3(weights)
    small = mm3(left, split3(moved_by(left)), True)
    small_parts = split3(small)
    turned = mm3(small_parts, left)
    identity = lax.broadcasted_iota(jnp.int32, small.shape, 0) == lax.broadcasted_iota(jnp.int32, small.shape, 1)
    scale = (jnp.sum(jnp.where(identity, small, 0.0), keepdims=True) + 1e-06) / rank
    weights = 1.5 * weights - 0.5 * turned / scale
    factor = jnp.where(identity, 1.5, 0.0) - 0.5 * small / scale
    norm_sq = jnp.sum(factor * mm3(split3(factor), small_parts), axis=1, keepdims=True)
    norm_sq = jnp.maximum(norm_sq, 0.0)
    value = jnp.sum(weights * picked, axis=1, keepdims=True)
    floor_value = 0.5 * jnp.sqrt(norm_sq / cells_all + 1e-06)
    sign = value / jnp.maximum(jnp.abs(value), floor_value)
    fields = out_ref.shape[0] // rank
    modes = mm3(split3(weights), tuple(parts_ref[i * total : (i + 1) * total] for i in range(3)))
    for f in range(fields):
        out_ref[pl.ds(f, rank, stride=fields), :] = modes[:, f * lanes : (f + 1) * lanes] * sign


def call(kernel, shapes, specs, *args, name, scratch=()):
    outs = jax.tree.map(lambda _: VMEM, shapes)
    return pl.pallas_call(
        kernel,
        out_shape=shapes,
        in_specs=specs,
        out_specs=outs,
        scratch_shapes=scratch,
        name=name,
        compiler_params=pltpu.CompilerParams(vmem_limit_bytes=20 * 2**20),
    )(*args)


def f32(*shape):
    return jax.ShapeDtypeStruct(shape, jnp.float32)


def exchange(value, axis):
    return lax.all_to_all(value, axis, 0, 0, tiled=True)


def child_maps(merge_rot, merge_order):
    rank = merge_rot.shape[2]
    swapped = jnp.where(merge_order[:, None, None] == 0, merge_rot, jnp.roll(merge_rot, rank, axis=1))
    children = swapped.reshape(-1, rank * rank)
    return jnp.pad(children, ((0, -children.shape[0] % 128), (0, 0)))


def local(velocity, block_id, metric, leaf_rot, merge_rot, merge_order, ref_cell):
    snaps, _, rows_y, cells_x, cells_z = velocity.shape
    rank = leaf_rot.shape[2]
    groups = lax.axis_size(SNAP)
    slabs = lax.axis_size("space")
    snap_index = lax.axis_index(SNAP)
    space_index = lax.axis_index("space")
    fields = 3 * rows_y
    total = groups * snaps
    plane = cells_x * cells_z

    per_x = fields * snaps
    packed = pl.pallas_call(
        pack_kernel,
        out_shape=jax.ShapeDtypeStruct((cells_x, per_x, cells_z), velocity.dtype),
        in_specs=[pl.BlockSpec(memory_space=pl.ANY)],
        out_specs=pl.BlockSpec(memory_space=pl.ANY),
        scratch_shapes=[
            pltpu.VMEM((3, snaps, rows_y, cells_x, cells_z), velocity.dtype),
            pltpu.VMEM((fields, cells_x * snaps, cells_z), jnp.float32),
            pltpu.VMEM((fields, cells_x, snaps, cells_z), velocity.dtype),
            pltpu.SemaphoreType.DMA((3,)),
            pltpu.SemaphoreType.DMA((fields,)),
        ],
        name="pack",
    )(velocity)
    own = exchange(packed, SNAP)

    levels = groups.bit_length() - 1
    rest_shape = (levels - 1, rank * rank, total)
    children = child_maps(merge_rot, merge_order)
    rest = pl.pallas_call(
        tables_kernel,
        out_shape=f32(*rest_shape),
        in_specs=[VMEM],
        out_specs=pl.BlockSpec(memory_space=pltpu.HBM),
        scratch_shapes=[pltpu.VMEM(rest_shape, jnp.float32), pltpu.SemaphoreType.DMA((levels - 1,))],
        name="tables",
    )(children)
    own_map = lax.dynamic_index_in_dim(children, snap_index, 0, keepdims=False).reshape(rank, rank)
    leaf = jnp.sum(own_map[:, :, None] * leaf_rot[0].T[:, None, :], axis=0).reshape(1, cells_z)
    rows_total = rows_y * slabs
    comp_of = ref_cell // (rows_total * plane)
    row_of = ref_cell // plane % rows_total - space_index * rows_y
    x_of = ref_cell % plane // cells_z
    here = (row_of >= 0) & (row_of < rows_y) & (x_of == snap_index)
    position = jnp.where(here, (comp_of * rows_y + row_of) * cells_z + ref_cell % cells_z, -1)
    position = position[:, None]
    ids = lax.dynamic_index_in_dim(block_id, snap_index, 1, keepdims=False)
    half = 0.5 * sum(
        jnp.where(ids[:, None] == b, metric[b][None, :, None], 0.0) for b in range(metric.shape[0])
    )
    at = jnp.arange(groups, dtype=jnp.int32)[:, None]
    origin = (space_index == 0) & (lax.axis_index("y") == 0)
    leaf_here = ((space_index == 0) & (at != 0)) | ((space_index == 1) & (at == 0))
    diagonal_here = ((space_index != 1) & (at == 0)) | ((space_index == 1) & (at == 1))
    marks = jnp.broadcast_to(diagonal_here.astype(jnp.float32), (groups, cells_z))
    side = jnp.concatenate([jnp.where(leaf_here, leaf, 0.0), marks], axis=0)
    origin = jnp.full((8, cells_z), origin, jnp.float32)
    own, rest, position, half, side, origin = lax.optimization_barrier((own, rest, position, half, side, origin))
    inner = own[:, snaps : 5 * snaps]
    is_even = space_index % 2 == 0
    low, high = own[:, : 2 * snaps], own[:, 4 * snaps :]
    swaps = [(i, i ^ 1) for i in range(slabs)]
    chip = lax.ppermute(jnp.where(is_even, high, low), "space", swaps)
    swaps = [(i, i - 1 if i % 2 == 0 else i + 1) for i in range(1, slabs - 1)]
    beyond = lax.ppermute(jnp.where(is_even, low, high), "space", swaps)
    even = jnp.full((8, cells_z), is_even, jnp.float32)
    left = lax.ppermute(inner, SNAP, [(i, (i + 1) % groups) for i in range(groups)])
    right = lax.ppermute(inner, SNAP, [((i + 1) % groups, i) for i in range(groups)])
    chunk = snaps + 2
    field_parts, table = call(
        gram_kernel,
        (jax.ShapeDtypeStruct((3 * total, fields * cells_z), BF16), f32(groups * chunk, cells_z)),
        [VMEM] * 9,
        half,
        position,
        own,
        left,
        right,
        chip,
        beyond,
        even,
        side,
        name="gram",
        scratch=[pltpu.VMEM((total, cells_z), jnp.float32)],
    )
    fold = [pltpu.VMEM((4 * chunk, cells_z), jnp.float32)]
    pieces = (groups, chunk // 2, 2, cells_z)
    table = exchange(table.reshape(pieces), WIDE).reshape(-1, cells_z)
    depth = lax.axis_size("z")
    table = call(
        sum_wide_kernel, f32(depth, 2 * snaps, cells_z), [VMEM] * 2, table, origin, name="sum_wide", scratch=fold
    )
    parts = exchange(table, "z")
    table = call(sum_z_kernel, f32(groups * chunk, cells_z), [VMEM], parts, name="sum_z", scratch=fold)
    table = exchange(table.reshape(pieces), WIDE).reshape(-1, cells_z)
    modes = call(
        functools.partial(tree_kernel, fields * plane * slabs),
        f32(rank * fields, cells_z),
        [VMEM] * 4,
        table,
        parts,
        rest,
        field_parts,
        name="tree",
        scratch=[pltpu.VMEM((total, cells_z), jnp.float32)],
    )
    return modes.reshape(rank, 3, rows_y, cells_z)


def solution(mesh):
    torus = jax.sharding.Mesh(mesh.devices.reshape(mesh.shape["space"], 4, -1), ("space", "y", "z"))
    placed = (
        P(SNAP, None, "space", None, None),
        P("space", None, None),
        P(),
        P(SNAP, None, None),
        P(),
        P(),
        P(),
    )
    return jax.shard_map(
        local, mesh=torus, in_specs=placed, out_specs=P(None, None, "space", SNAP), check_vma=False
    )
```

```python
import functools

import jax
import jax.numpy as jnp
from jax import lax
from jax.experimental import pallas as pl
from jax.experimental.pallas import tpu as pltpu
from jax.sharding import PartitionSpec as P

HIGHEST = lax.Precision.HIGHEST
VMEM = pl.BlockSpec(memory_space=pltpu.VMEM)
SNAP = ("y", "z")
WIDE = ("space", "y")


BF16 = jnp.bfloat16


def split3(value):
    high = value.astype(BF16)
    rest = value - high.astype(jnp.float32)
    middle = rest.astype(BF16)
    low = (rest - middle.astype(jnp.float32)).astype(BF16)
    return high, middle, low


def dot(left, right, transposed=False):
    dims = (((1,), (1 if transposed else 0,)), ((), ()))
    return lax.dot_general(left, right, dims, preferred_element_type=jnp.float32)


def mm3(left, right, transposed=False):
    rows = left[0].shape[0]
    high = dot(jnp.concatenate(left, axis=0), right[0], transposed)
    middle = dot(jnp.concatenate(left[:2], axis=0), right[1], transposed)
    low = dot(left[0], right[2], transposed)
    small = low + middle[rows:] + high[2 * rows :]
    return small + (middle[:rows] + high[rows : 2 * rows]) + high[:rows]


SLOTS = {(0, 0): 0, (2, 0): 1, (1, 0): 2, (1, 1): 3, (2, 1): 4, (0, 1): 5}


def pack_kernel(vel_hbm, out_hbm, vel_ref, rows_ref, out_ref, in_sems, out_sems):
    snaps, comps, rows_y, cells_x, lanes = vel_hbm.shape
    arrivals, leaving = {}, []
    for c in range(comps):
        arrivals[c] = pltpu.make_async_copy(vel_hbm.at[:, c], vel_ref.at[c], in_sems.at[c])
        arrivals[c].start()
    for (c, y), slot in sorted(SLOTS.items()):
        if y == 0:
            arrivals[c].wait()
        for s in range(snaps):
            rows_ref[slot, pl.ds(s, cells_x, stride=snaps), :] = vel_ref[c, s, y].astype(jnp.float32)
        out_ref[slot] = rows_ref[slot].reshape(cells_x, snaps, lanes).astype(out_ref.dtype)
        target = out_hbm.at[:, pl.ds(slot * snaps, snaps)]
        leaving.append(pltpu.make_async_copy(out_ref.at[slot], target, out_sems.at[slot]))
        leaving[-1].start()
    for copy in leaving:
        copy.wait()


def gram_kernel(
    half_ref, ref_pos_ref, own_ref, left_ref, right_ref, chip_ref, next_ref, even_ref, side_ref,
    parts_ref, out_ref, table_ref
):
    groups, per_x, lanes = own_ref.shape
    rows_y = half_ref.shape[0]
    fields = 3 * rows_y
    snaps = per_x // fields
    total = groups * snaps

    def rows(ref, slot):
        return ref[:, slot * snaps : (slot + 1) * snaps, :].astype(jnp.float32).reshape(total, lanes)

    def diff_z(field):
        return pltpu.roll(field, lanes - 1, 1) - pltpu.roll(field, 1, 1)

    def diff_x(c, y):
        slot = SLOTS[c, y] - 1
        return rows(right_ref, slot) - rows(left_ref, slot)

    u, v, w = ([rows(own_ref, SLOTS[c, y]) for y in range(rows_y)] for c in range(3))
    even = even_ref[:1] > 0
    chip = [rows(chip_ref, i) for i in range(2)]
    beyond = [rows(next_ref, i) for i in range(2)]
    u_all = [jnp.where(even, beyond[1], chip[1])] + u + [jnp.where(even, chip[0], beyond[0])]
    w_all = [jnp.where(even, beyond[0], chip[0])] + w + [jnp.where(even, chip[1], beyond[1])]
    pieces = [None] * fields
    for y in range(rows_y):
        half = (half_ref[y, k : k + 1] for k in range(3))
        hx, hy, hz = half
        pieces[y] = hy * (w_all[y + 2] - w_all[y]) - hz * diff_z(v[y])
        pieces[rows_y + y] = hz * diff_z(u[y]) - hx * diff_x(2, y)
        pieces[2 * rows_y + y] = hx * diff_x(1, y) - hy * (u_all[y + 2] - u_all[y])
    for f, piece in enumerate(pieces):
        for i, part in enumerate(split3(piece)):
            parts_ref[i * total : (i + 1) * total, f * lanes : (f + 1) * lanes] = part

    count = ref_pos_ref.shape[0]
    hot = lax.broadcasted_iota(jnp.int32, (count, fields * lanes), 1) == ref_pos_ref[...]
    hot = hot.astype(jnp.float32).astype(BF16)

    def against(rows, part):
        streamed = jnp.concatenate([hot, parts_ref[:rows]], axis=0)
        result = dot(streamed, parts_ref[part * total : (part + 1) * total], True)
        return result[:count], result[count:]

    picked_high, high = against(3 * total, 0)
    picked_middle, middle = against(2 * total, 1)
    picked_low, low = against(total, 2)
    picked = picked_low + picked_middle + picked_high
    gram = low + middle[total:] + high[2 * total :]
    gram = gram + (middle[:total] + high[total : 2 * total]) + high[:total]
    h = total // 2
    row = lax.broadcasted_iota(jnp.int32, (h, h), 0)
    col = lax.broadcasted_iota(jnp.int32, (h, h), 1)
    last = gram[h:, h:]
    diagonal = jnp.sum(jnp.where(row == col, last, 0.0), axis=0, keepdims=True)
    table_ref[:h] = jnp.where(row <= col, gram[:h, :h], last)
    table_ref[h:] = gram[:h, h:]
    chunk = snaps + 2
    for r in range(snaps):
        out_ref[pl.ds(r, groups, stride=chunk), :] = table_ref[pl.ds(r, groups, stride=snaps), :]
    out_ref[pl.ds(snaps, groups, stride=chunk), :] = jnp.concatenate([picked[:, :h], picked[:, h:]], axis=0)
    side = side_ref[:groups] + jnp.where(side_ref[groups:] > 0, diagonal, 0.0)
    out_ref[pl.ds(snaps + 1, groups, stride=chunk), :] = side


def sum_wide_kernel(parts_ref, origin_ref, out_ref, fold_ref):
    copies, rows, lanes = out_ref.shape
    sources = 32
    chunk = parts_ref.shape[0] // sources
    block = 4 * chunk
    total = parts_ref[:block]
    for i in range(1, sources // 4):
        total = total + parts_ref[i * block : (i + 1) * block]
    fold_ref[...] = total
    total = sum(fold_ref[i * chunk : (i + 1) * chunk] for i in range(4))
    side = parts_ref[pl.ds(chunk - 1, sources, stride=chunk), :]
    origin = origin_ref[:1] > 0
    leaves = jnp.where(origin, side[4:8], side[:4])
    row = lax.broadcasted_iota(jnp.int32, side.shape, 0)
    second = (row >= 4) & (row < 8)
    diagonal = jnp.where(second, 0.0, side), jnp.where(second, side, 0.0)
    diagonal = [jnp.sum(value, axis=0, keepdims=True) for value in diagonal]
    out_ref[0, : chunk - 1] = total[: chunk - 1]
    out_ref[0, chunk - 1 : chunk] = jnp.where(origin, diagonal[0], diagonal[1])
    out_ref[0, chunk : chunk + 4] = leaves
    out_ref[0, chunk + 4 :] = jnp.zeros((rows - chunk - 4, lanes), jnp.float32)
    whole = out_ref[0]
    for i in range(1, copies):
        out_ref[i] = whole


def sum_z_kernel(parts_ref, out_ref, fold_ref):
    block = fold_ref.shape[0]
    chunk = block // 4
    total = jnp.sum(parts_ref[...], axis=0)[:chunk]
    for i in range(4):
        fold_ref[i * chunk : (i + 1) * chunk] = total
    whole = fold_ref[...]
    for i in range(out_ref.shape[0] // block):
        out_ref[i * block : (i + 1) * block] = whole


def tables_kernel(children_ref, rest_hbm, rest_ref, sems):
    count, size, total = rest_hbm.shape
    tables = jnp.concatenate(split3(children_ref[...].T), axis=0)
    width = tables.shape[1]
    child = lax.broadcasted_iota(jnp.int32, (width, total), 0)
    snap = lax.broadcasted_iota(jnp.int32, (width, total), 1)
    span = total >> count
    first = 2 * (total // span)
    copies = []
    for level in range(count):
        chosen = (child == first + snap // span).astype(jnp.float32).astype(BF16)
        first, span = first + total // span, span * 2
        spread = dot(tables, chosen)
        rest_ref[level] = spread[:size] + spread[size : 2 * size] + spread[2 * size :]
        copies.append(pltpu.make_async_copy(rest_ref.at[level], rest_hbm.at[level], sems.at[level]))
        copies[-1].start()
    for copy in copies:
        copy.wait()


def leaf_weights(pieces_ref, rank, total):
    lanes = pieces_ref.shape[2]
    snaps = lanes // rank
    leaves = jnp.concatenate([pieces_ref[:, snaps + 2 + i] for i in range(4)], axis=0)
    groups = leaves.shape[0]
    own_group = lax.broadcasted_iota(jnp.int32, (groups, total), 0)
    own_group = own_group == lax.broadcasted_iota(jnp.int32, (groups, total), 1) // snaps
    wide = dot(jnp.concatenate(split3(leaves.T), axis=0), own_group.astype(jnp.float32).astype(BF16))
    wide = wide[:lanes] + wide[lanes : 2 * lanes] + wide[2 * lanes :]
    row = lax.broadcasted_iota(jnp.int32, wide.shape, 0)
    col = lax.broadcasted_iota(jnp.int32, wide.shape, 1)
    return jnp.sum(jnp.where(row % snaps == col % snaps, wide, 0.0).reshape(rank, snaps, total), axis=1)


def rotated(weights, rotate_ref):
    rank = weights.shape[0]
    total = rotate_ref[:rank] * weights[:1]
    for a in range(1, rank):
        total = total + rotate_ref[a * rank : (a + 1) * rank] * weights[a : a + 1]
    return total


def tree_kernel(
    cells_all, table_ref, pieces_ref, rest_ref, parts_ref, out_ref, packed_ref
):
    total = rest_ref.shape[2]
    lanes = table_ref.shape[1]
    rank = out_ref.shape[0] * lanes // parts_ref.shape[1]
    h = total // 2
    snaps = lanes // rank
    groups = total // snaps
    chunk = snaps + 2
    for r in range(snaps):
        packed_ref[pl.ds(r, groups, stride=snaps), :] = table_ref[pl.ds(r, groups, stride=chunk), :]
    picked = table_ref[pl.ds(snaps, groups, stride=chunk), :]
    picked = jnp.concatenate([picked[:rank], picked[rank:]], axis=1)
    last_diag = table_ref[chunk - 1 : chunk] + table_ref[2 * chunk - 1 : 2 * chunk]
    mixed = packed_ref[:h]
    cross = packed_ref[h:]
    mixed_t = mixed.T
    row = lax.broadcasted_iota(jnp.int32, (h, h), 0)
    col = lax.broadcasted_iota(jnp.int32, (h, h), 1)
    first = jnp.where(row <= col, mixed, mixed_t)
    last = jnp.where(row > col, mixed, jnp.where(row == col, last_diag, mixed_t))
    first = split3(first)
    last = split3(last)
    cross = split3(cross)

    cross_t = split3(packed_ref[h:].T)
    whole = tuple(
        jnp.concatenate([jnp.concatenate([f, c], axis=1), jnp.concatenate([t, l], axis=1)], axis=0)
        for f, c, t, l in zip(first, cross, cross_t, last)
    )

    row_all = lax.broadcasted_iota(jnp.int32, (total, total), 0)
    col_all = lax.broadcasted_iota(jnp.int32, (total, total), 1)
    weights = leaf_weights(pieces_ref, rank, total)
    levels = groups.bit_length() - 1
    for level in range(levels - 1):
        span = 2 * snaps << level
        if level:
            weights = rotated(weights, rest_ref.at[level - 1])
        left = split3(weights)
        same = (row_all // span == col_all // span).astype(jnp.float32).astype(BF16)
        inside = same[:h, :h]
        begin = mm3(tuple(part[:, :h] for part in left), tuple(part * inside for part in first))
        end = mm3(tuple(part[:, h:] for part in left), tuple(part * inside for part in last))
        moved = jnp.concatenate([begin, end], axis=1)
        own = jnp.sum(weights * moved, axis=0, keepdims=True)
        products = [weights[j : j + 1] * moved for j in range(rank)]
        products = jnp.concatenate(products + [jnp.broadcast_to(own, (rank, total))], axis=0)
        upper = products.astype(BF16)
        lower = (products - upper.astype(jnp.float32)).astype(BF16)
        count = products.shape[0]
        sums = dot(jnp.concatenate([upper, lower], axis=0), same)
        sums = sums[count:] + sums[:count]
        share = 0.5 * rank / (sums[rank * rank :] + 1e-06)
        turned = sums[:rank] * weights[:1]
        for j in range(1, rank):
            turned = turned + sums[j * rank : (j + 1) * rank] * weights[j : j + 1]
        weights = 1.5 * weights - turned * share

    weights = rotated(weights, rest_ref.at[levels - 2])
    left = split3(weights)
    small = mm3(left, split3(mm3(left, whole)), True)
    small_parts = split3(small)
    turned = mm3(small_parts, left)
    identity = lax.broadcasted_iota(jnp.int32, small.shape, 0) == lax.broadcasted_iota(jnp.int32, small.shape, 1)
    scale = (jnp.sum(jnp.where(identity, small, 0.0), keepdims=True) + 1e-06) / rank
    weights = 1.5 * weights - 0.5 * turned / scale
    factor = jnp.where(identity, 1.5, 0.0) - 0.5 * small / scale
    norm_sq = jnp.sum(factor * mm3(split3(factor), small_parts), axis=1, keepdims=True)
    norm_sq = jnp.maximum(norm_sq, 0.0)
    value = jnp.sum(weights * picked, axis=1, keepdims=True)
    floor_value = 0.5 * jnp.sqrt(norm_sq / cells_all + 1e-06)
    sign = value / jnp.maximum(jnp.abs(value), floor_value)
    fields = out_ref.shape[0] // rank
    modes = mm3(split3(weights), tuple(parts_ref[i * total : (i + 1) * total] for i in range(3)))
    for f in range(fields):
        out_ref[pl.ds(f, rank, stride=fields), :] = modes[:, f * lanes : (f + 1) * lanes] * sign


def call(kernel, shapes, specs, *args, name, scratch=()):
    outs = jax.tree.map(lambda _: VMEM, shapes)
    return pl.pallas_call(
        kernel,
        out_shape=shapes,
        in_specs=specs,
        out_specs=outs,
        scratch_shapes=scratch,
        name=name,
        compiler_params=pltpu.CompilerParams(vmem_limit_bytes=20 * 2**20),
    )(*args)


def f32(*shape):
    return jax.ShapeDtypeStruct(shape, jnp.float32)


def exchange(value, axis):
    return lax.all_to_all(value, axis, 0, 0, tiled=True)


def child_maps(merge_rot, merge_order):
    rank = merge_rot.shape[2]
    swapped = jnp.where(merge_order[:, None, None] == 0, merge_rot, jnp.roll(merge_rot, rank, axis=1))
    children = swapped.reshape(-1, rank * rank)
    return jnp.pad(children, ((0, -children.shape[0] % 128), (0, 0)))


def local(velocity, block_id, metric, leaf_rot, merge_rot, merge_order, ref_cell):
    snaps, _, rows_y, cells_x, cells_z = velocity.shape
    rank = leaf_rot.shape[2]
    groups = lax.axis_size(SNAP)
    slabs = lax.axis_size("space")
    snap_index = lax.axis_index(SNAP)
    space_index = lax.axis_index("space")
    fields = 3 * rows_y
    total = groups * snaps
    plane = cells_x * cells_z

    per_x = fields * snaps
    packed = pl.pallas_call(
        pack_kernel,
        out_shape=jax.ShapeDtypeStruct((cells_x, per_x, cells_z), velocity.dtype),
        in_specs=[pl.BlockSpec(memory_space=pl.ANY)],
        out_specs=pl.BlockSpec(memory_space=pl.ANY),
        scratch_shapes=[
            pltpu.VMEM((3, snaps, rows_y, cells_x, cells_z), velocity.dtype),
            pltpu.VMEM((fields, cells_x * snaps, cells_z), jnp.float32),
            pltpu.VMEM((fields, cells_x, snaps, cells_z), velocity.dtype),
            pltpu.SemaphoreType.DMA((3,)),
            pltpu.SemaphoreType.DMA((fields,)),
        ],
        name="pack",
    )(velocity)
    own = exchange(packed, SNAP)

    levels = groups.bit_length() - 1
    rest_shape = (levels - 1, rank * rank, total)
    children = child_maps(merge_rot, merge_order)
    rest = pl.pallas_call(
        tables_kernel,
        out_shape=f32(*rest_shape),
        in_specs=[VMEM],
        out_specs=pl.BlockSpec(memory_space=pltpu.HBM),
        scratch_shapes=[pltpu.VMEM(rest_shape, jnp.float32), pltpu.SemaphoreType.DMA((levels - 1,))],
        name="tables",
    )(children)
    own_map = lax.dynamic_index_in_dim(children, snap_index, 0, keepdims=False).reshape(rank, rank)
    leaf = jnp.sum(own_map[:, :, None] * leaf_rot[0].T[:, None, :], axis=0).reshape(1, cells_z)
    rows_total = rows_y * slabs
    comp_of = ref_cell // (rows_total * plane)
    row_of = ref_cell // plane % rows_total - space_index * rows_y
    x_of = ref_cell % plane // cells_z
    here = (row_of >= 0) & (row_of < rows_y) & (x_of == snap_index)
    position = jnp.where(here, (comp_of * rows_y + row_of) * cells_z + ref_cell % cells_z, -1)
    position = position[:, None]
    ids = lax.dynamic_index_in_dim(block_id, snap_index, 1, keepdims=False)
    half = 0.5 * sum(
        jnp.where(ids[:, None] == b, metric[b][None, :, None], 0.0) for b in range(metric.shape[0])
    )
    at = jnp.arange(groups, dtype=jnp.int32)[:, None]
    origin = (space_index == 0) & (lax.axis_index("y") == 0)
    leaf_here = ((space_index == 0) & (at != 0)) | ((space_index == 1) & (at == 0))
    diagonal_here = ((space_index != 1) & (at == 0)) | ((space_index == 1) & (at == 1))
    marks = jnp.broadcast_to(diagonal_here.astype(jnp.float32), (groups, cells_z))
    side = jnp.concatenate([jnp.where(leaf_here, leaf, 0.0), marks], axis=0)
    origin = jnp.full((8, cells_z), origin, jnp.float32)
    own, rest, position, half, side, origin = lax.optimization_barrier((own, rest, position, half, side, origin))
    inner = own[:, snaps : 5 * snaps]
    is_even = space_index % 2 == 0
    low, high = own[:, : 2 * snaps], own[:, 4 * snaps :]
    swaps = [(i, i ^ 1) for i in range(slabs)]
    chip = lax.ppermute(jnp.where(is_even, high, low), "space", swaps)
    swaps = [(i, i - 1 if i % 2 == 0 else i + 1) for i in range(1, slabs - 1)]
    beyond = lax.ppermute(jnp.where(is_even, low, high), "space", swaps)
    even = jnp.full((8, cells_z), is_even, jnp.float32)
    left = lax.ppermute(inner, SNAP, [(i, (i + 1) % groups) for i in range(groups)])
    right = lax.ppermute(inner, SNAP, [((i + 1) % groups, i) for i in range(groups)])
    chunk = snaps + 2
    field_parts, table = call(
        gram_kernel,
        (jax.ShapeDtypeStruct((3 * total, fields * cells_z), BF16), f32(groups * chunk, cells_z)),
        [VMEM] * 9,
        half,
        position,
        own,
        left,
        right,
        chip,
        beyond,
        even,
        side,
        name="gram",
        scratch=[pltpu.VMEM((total, cells_z), jnp.float32)],
    )
    fold = [pltpu.VMEM((4 * chunk, cells_z), jnp.float32)]
    pieces = (groups, chunk // 2, 2, cells_z)
    table = exchange(table.reshape(pieces), WIDE).reshape(-1, cells_z)
    depth = lax.axis_size("z")
    table = call(
        sum_wide_kernel, f32(depth, 2 * snaps, cells_z), [VMEM] * 2, table, origin, name="sum_wide", scratch=fold
    )
    parts = exchange(table, "z")
    table = call(sum_z_kernel, f32(groups * chunk, cells_z), [VMEM], parts, name="sum_z", scratch=fold)
    table = exchange(table.reshape(pieces), WIDE).reshape(-1, cells_z)
    modes = call(
        functools.partial(tree_kernel, fields * plane * slabs),
        f32(rank * fields, cells_z),
        [VMEM] * 4,
        table,
        parts,
        rest,
        field_parts,
        name="tree",
        scratch=[pltpu.VMEM((total, cells_z), jnp.float32)],
    )
    return modes.reshape(rank, 3, rows_y, cells_z)


def solution(mesh):
    torus = jax.sharding.Mesh(mesh.devices.reshape(mesh.shape["space"], 4, -1), ("space", "y", "z"))
    placed = (
        P(SNAP, None, "space", None, None),
        P("space", None, None),
        P(),
        P(SNAP, None, None),
        P(),
        P(),
        P(),
    )
    return jax.shard_map(
        local, mesh=torus, in_specs=placed, out_specs=P(None, None, "space", SNAP), check_vma=False
    )
```
